32 devices in a mesh: dp: 4 (over z), expert: 8 (over y, x, core).
Axes of the slice: x: 2, y: 2, z: 4, core: 2. Of those that a mesh axis runs over, the one named last changes fastest.
Arguments:
- residual: bfloat16 [4096, 1280], P(('dp', 'expert')), may hold values from -6 to 6
- context: bfloat16 [4096, 1280], P(('dp', 'expert')), may hold values from -6 to 6
- w_out: bfloat16 [1280, 1280], P(('dp', 'expert')), may hold values from -0.15625 to 0.15625
- w_router: bfloat16 [1280, 16], replicated, may hold values from -0.15625 to 0.15625
- expert_ids: int32 [4096, 2], P(('dp', 'expert')), may hold values from 0 to 15, all different within a row; in each aligned block of 128 rows (0 to 127, 128 to 255, ...) at most 20 rows name the same one
- w_fc1: bfloat16 [16, 1280, 5120], P('expert', None, 'dp'), may hold values from -0.15625 to 0.15625
- w_fc2: bfloat16 [16, 5120, 1280], P('expert', 'dp'), may hold values from -0.078125 to 0.078125
- cotangent: bfloat16 [4096, 1280], P(('dp', 'expert')), may hold values from -6 to 6
Outputs:
- layer_out: bfloat16 [4096, 1280], P(('dp', 'expert'))
- d_residual: bfloat16 [4096, 1280], P(('dp', 'expert'))
- d_context: bfloat16 [4096, 1280], P(('dp', 'expert'))
- grad_out: float32 [1280, 1280], P(('dp', 'expert'))
- grad_router: float32 [1280, 16], P(('dp', 'expert'))
- grad_fc1: float32 [16, 1280, 5120], P('expert', None, 'dp')
- grad_fc2: float32 [16, 5120, 1280], P('expert', 'dp')
The draws below stay inside these ranges and needn't reach their ends.
Inputs may be any that keep to these rules, and one draw needn't show every extreme that they name: `expert_ids`: each row names 2 different experts. Among the 128 rows of one device no expert is named more than 20 times, and some device has an expert named exactly 20 times.
All inputs are finite; a program needn't handle non-finite values.
Results may differ from the reference program's by a relative error of at most 0.01.
Values may be sent and summed in bfloat16 or wider, within the bound.
No kernel may reach another device: no remote copies, remote signals or barrier semaphores. Data moves between devices by JAX's collectives and lax.ppermute only.
A program may use at most 192 MiB of HBM per device.

```python
import math
import jax
import jax.numpy as jnp
import numpy as np
from jax import lax

D = 1280
FF = 5120
TOP = 2
TOK_DEV = 128
EXPERTS = 16
TOKENS = 4096
CAP = 20
N_DP = 4
N_EXPERT = 8


def strengthened(values, own_key, source, target, blocks, factor):
    owner, partner = [(jnp.arange(values.shape[axis_at]) // (values.shape[axis_at] // blocks)).reshape([-1 if axis == axis_at else 1 for axis in range(values.ndim)]) for axis_at in (source, target)]
    chosen = jax.random.permutation(own_key, blocks)[partner]
    strong = (owner == chosen) | (owner == (partner + blocks // 2) % blocks)
    return jnp.where(strong, factor * values, values)


def shard_levels(own_key, extent, shards, least, high):
    def one(axis_at, parts):
        heights = jax.random.uniform(jax.random.fold_in(jax.random.fold_in(own_key, 6), axis_at), (parts,), jnp.float32, least / len(shards), high / len(shards))
        return jnp.repeat(jnp.exp(heights), extent[axis_at] // parts).reshape((-1,) + (1,) * (len(extent) - axis_at - 1))

    loudness = one(*shards[0])
    for cut in shards[1:]:
        loudness = loudness * one(*cut)
    return loudness


def shared_out(key, own, number, rows, count, top, limit, skew):
    sequence = jax.random.permutation(key, count)
    packed, common = load_shares(count, rows * top, limit, skew, True), load_shares(count, rows * top, limit, skew, False)
    places = jnp.arange(count)

    def named(sizes, offset_by):
        used = int((sizes > 0).sum())
        fixed = max(1, used // 4)
        shifted = fixed + (places - fixed + offset_by * (used - fixed)) % max(1, count - fixed)
        return jnp.zeros((count,), jnp.int32).at[sequence[jnp.where(places < fixed, places, shifted)]].set(jnp.asarray(sizes, jnp.int32))

    sizes = jnp.where(number % 4 == 0, named(packed, number // 4), named(common, number - number // 4 - 1))
    mixed = jax.random.permutation(jax.random.fold_in(own, 3), count)
    source_of, sink = mixed[0:count // 2 * 2:2], mixed[1:count // 2 * 2:2]
    margin = jnp.minimum(sizes[source_of] - 1, limit - sizes[sink]) // 2
    margin = jnp.where((source_of == sequence[0]) | (sink == sequence[0]) | (sizes[sink] == 0), 0, jnp.maximum(margin, 0))
    shifted = jax.random.randint(jax.random.fold_in(own, 4), (count // 2,), 0, 1 << 20) % (margin + 1)
    sizes = sizes.at[source_of].add(-shifted).at[sink].add(shifted)
    labels = jnp.searchsorted(jnp.cumsum(sizes), jnp.arange(rows * top), side="right").astype(jnp.int32)
    listing = labels.reshape(top, rows).T
    listing = listing[jax.random.permutation(jax.random.fold_in(own, 1), rows)]
    offset_by = jax.random.randint(jax.random.fold_in(own, 2), (rows, 1), 0, top)
    return jnp.take_along_axis(listing, (jnp.arange(top)[None, :] + offset_by) % top, axis=1)


def load_shares(amount, total, limit, slope, full):
    loads = [(1 << 20) // math.isqrt(standing ** slope) + 1 for standing in range(1, amount + 1)]
    largest = limit if full else min(limit, max(-(-total // amount), total * loads[0] // sum(loads)))
    least = 1 if total - largest >= amount - 1 else 0
    holding, surplus = [largest] + [least] * (amount - 1), total - largest - least * (amount - 1)
    while surplus > 0:
        movable = [i for i in range(1, amount) if holding[i] < largest] or [i for i in range(1, amount) if holding[i] < limit]
        whole, left = sum([loads[i] for i in movable]), surplus
        for i in movable:
            more = min(limit - holding[i], max(1, left * loads[i] // whole), surplus)
            holding[i] = holding[i] + more
            surplus = surplus - more
    return np.array(holding)


def bell_draw(rng, shape, scale, reach, cuts=(), held_as=jnp.bfloat16):
    entries = scale * jax.random.normal(rng, shape, jnp.float32)
    if cuts:
        entries = entries * shard_levels(rng, shape, cuts, -0.22, 0.18)
    return jnp.clip(entries, -reach, reach).astype(held_as)


def bell_draw_with(key, shape, width, bound, cuts, heavy, kind=jnp.bfloat16):
    entries = width * jax.random.normal(key, shape, jnp.float32)
    if cuts:
        entries = entries * shard_levels(key, shape, cuts, -0.22, 0.18)
    return jnp.clip(strengthened(entries, jax.random.fold_in(key, 3), *heavy), -bound, bound).astype(kind)


def setup_inputs(seed: int = 0) -> dict:
    key_list = jax.random.split(jax.random.key(seed), 9)
    residual = bell_draw(key_list[0], (TOKENS, D), 1.0, 6.0, ((0, 32),))
    context = bell_draw_with(key_list[1], (TOKENS, D), 1.0, 6.0, ((0, 32),), (0, 1, 32, 2.75))
    w_out = bell_draw(key_list[2], (D, D), D ** -0.5, 0.15625, ((0, 32),))
    w_router = bell_draw(key_list[3], (D, EXPERTS), D ** -0.5, 0.15625)
    expert_ids_keys = jax.random.split(jax.random.fold_in(key_list[4], 1), TOKENS // TOK_DEV)
    expert_ids_turns = jax.random.permutation(jax.random.fold_in(key_list[4], 3), TOKENS // TOK_DEV)
    expert_ids = jax.vmap(lambda own, number: shared_out(jax.random.fold_in(key_list[4], 2), own, number, TOK_DEV, EXPERTS, TOP, CAP, 1))(expert_ids_keys, expert_ids_turns).reshape((TOKENS, TOP))
    w_fc1 = bell_draw(key_list[5], (EXPERTS, D, FF), D ** -0.5, 0.15625, ((0, 8), (2, 4)))
    w_fc2 = bell_draw(key_list[6], (EXPERTS, FF, D), FF ** -0.5, 0.078125, ((0, 8), (1, 4)))
    cotangent = bell_draw(key_list[7], (TOKENS, D), 1.0, 6.0, ((0, 32),))
    return dict(residual=residual, context=context, w_out=w_out, w_router=w_router, expert_ids=expert_ids, w_fc1=w_fc1, w_fc2=w_fc2, cotangent=cotangent)


LN_EPS = 1e-06

def normal_cdf(value):
    return 0.5 * (1.0 + lax.erf(value * 0.7071067811865476))

def gelu_act(value):
    return value * normal_cdf(value)

def gelu_slope(value):
    return normal_cdf(value) + value * jnp.exp(-0.5 * value * value) * 0.3989422804014327

def block_slots(flat_ids):
    expert_iota = jnp.arange(EXPERTS, dtype=jnp.int32)
    onehot = (flat_ids[:, None] == expert_iota[None, :]).astype(jnp.int32)
    before = jnp.cumsum(onehot, axis=0) - onehot
    position = lax.optimization_barrier(jnp.sum(before * onehot, axis=1)).astype(jnp.int32)
    pair_ids = jnp.arange(TOK_DEV * TOP, dtype=jnp.int32)
    empty = jnp.full((EXPERTS, CAP), TOK_DEV * TOP, dtype=jnp.int32)
    return empty.at[flat_ids, position].set(pair_ids)

def rounded_sum(partials):
    rounded = lax.optimization_barrier(partials.astype(jnp.bfloat16))
    return lax.optimization_barrier(jnp.sum(rounded.astype(jnp.float32), axis=0))

def reference(residual, context, w_out, w_router, expert_ids, w_fc1, w_fc2, cotangent):
    devices = N_DP * N_EXPERT
    pair_count = TOK_DEV * TOP
    group_width = FF // N_DP
    grad_scale = float(TOKENS) ** (-0.5)
    stream = residual.astype(jnp.float32) + jnp.dot(context, w_out, preferred_element_type=jnp.float32)
    average = lax.optimization_barrier(jnp.mean(stream, axis=1, keepdims=True))
    centred = stream - average
    variance = lax.optimization_barrier(jnp.mean(centred * centred, axis=1, keepdims=True))
    inv_std = lax.rsqrt(variance + LN_EPS)
    normed = centred * inv_std
    normed_bf = normed.astype(jnp.bfloat16)
    logits = jnp.dot(normed_bf, w_router, preferred_element_type=jnp.float32)
    chosen = jnp.take_along_axis(logits, expert_ids, axis=1)
    gate_probs = jax.nn.sigmoid(chosen - chosen[:, ::-1])
    flat_gates = gate_probs.reshape(-1)
    tables = jax.vmap(block_slots)(expert_ids.reshape(devices, pair_count))
    block_base = (jnp.arange(devices, dtype=jnp.int32) * pair_count)[:, None]

    def expert_step(totals, expert_item):
        mixture, back_sum, d_gate = totals
        slot_table, first_w, second_w = expert_item
        is_live = (slot_table < pair_count).reshape(-1)
        pair_ids = (block_base + jnp.minimum(slot_table, pair_count - 1)).reshape(-1).astype(jnp.int32)
        token_ids = (pair_ids // TOP).astype(jnp.int32)
        slot_in = jnp.where(is_live[:, None], normed_bf[token_ids], jnp.zeros((), jnp.bfloat16))
        slot_gate = jnp.where(is_live, flat_gates[pair_ids], jnp.zeros((), jnp.float32))
        cot_rows = cotangent[token_ids].astype(jnp.float32)
        slot_cot = (slot_gate[:, None] * cot_rows).astype(jnp.bfloat16)
        preact = jnp.dot(slot_in, first_w, preferred_element_type=jnp.float32)
        hidden = gelu_act(preact).astype(jnp.bfloat16)
        slot_rows = hidden.shape[0]
        out_parts = jnp.einsum('rgh,ghd->grd', hidden.reshape(slot_rows, N_DP, group_width).astype(jnp.float32), second_w.reshape(N_DP, group_width, D).astype(jnp.float32))
        slot_out = rounded_sum(out_parts).astype(jnp.bfloat16)
        d_hidden = jnp.dot(slot_cot, second_w.T, preferred_element_type=jnp.float32)
        d_preact = (d_hidden * gelu_slope(preact)).astype(jnp.bfloat16)
        back_parts = jnp.einsum('rgh,dgh->grd', d_preact.reshape(slot_rows, N_DP, group_width).astype(jnp.float32), first_w.reshape(D, N_DP, group_width).astype(jnp.float32))
        slot_back = rounded_sum(back_parts).astype(jnp.bfloat16)
        grad_first = grad_scale * jnp.dot(slot_in.T, d_preact, preferred_element_type=jnp.float32)
        grad_second = grad_scale * jnp.dot(hidden.T, slot_cot, preferred_element_type=jnp.float32)
        target = jnp.where(is_live, token_ids, TOKENS).astype(jnp.int32)
        out_float = slot_out.astype(jnp.float32)
        mixture = mixture.at[target].add(slot_gate[:, None] * out_float, mode='drop')
        back_sum = back_sum.at[target].add(slot_back.astype(jnp.float32), mode='drop')
        gate_target = jnp.where(is_live, pair_ids, TOKENS * TOP).astype(jnp.int32)
        d_gate = d_gate.at[gate_target].set(lax.optimization_barrier(jnp.sum(cot_rows * out_float, axis=1)), mode='drop')
        return ((mixture, back_sum, d_gate), (grad_first, grad_second))
    initial = (jnp.zeros((TOKENS, D), jnp.float32), jnp.zeros((TOKENS, D), jnp.float32), jnp.zeros((TOKENS * TOP,), jnp.float32))
    totals, grads = lax.scan(expert_step, initial, (jnp.transpose(tables, (1, 0, 2)), w_fc1, w_fc2))
    mixture, back_sum, d_gate = totals
    grad_fc1, grad_fc2 = grads
    layer_out = (stream + mixture).astype(jnp.bfloat16)
    d_gate = d_gate.reshape(TOKENS, TOP)
    d_chosen = gate_probs * (d_gate - lax.optimization_barrier(jnp.sum(gate_probs * d_gate, axis=1, keepdims=True)))
    picked = (expert_ids[:, :, None] == jnp.arange(EXPERTS, dtype=jnp.int32)[None, None, :]).astype(jnp.float32)
    d_logits = lax.optimization_barrier(jnp.sum(picked * d_chosen[:, :, None], axis=1))
    d_normed = back_sum + jnp.dot(d_logits, w_router.astype(jnp.float32).T, precision=lax.Precision.HIGHEST)
    d_stream = cotangent.astype(jnp.float32) + inv_std * (d_normed - lax.optimization_barrier(jnp.mean(d_normed, axis=1, keepdims=True)) - normed * lax.optimization_barrier(jnp.mean(d_normed * normed, axis=1, keepdims=True)))
    d_residual = d_stream.astype(jnp.bfloat16)
    d_context = jnp.dot(d_residual, w_out.T, preferred_element_type=jnp.float32).astype(jnp.bfloat16)
    grad_out = grad_scale * jnp.dot(context.T, d_residual, preferred_element_type=jnp.float32)
    grad_router = grad_scale * jnp.dot(normed_bf.astype(jnp.float32).T, d_logits, precision=lax.Precision.HIGHEST)
    return (layer_out, d_residual, d_context, grad_out, grad_router, grad_fc1, grad_fc2)
```

```python
import functools

import jax
import jax.numpy as jnp
from jax import lax
from jax.experimental import pallas as pl
from jax.experimental.pallas import tpu as pltpu
from jax.sharding import PartitionSpec as P

from jax.experimental.layout import Layout, with_layout_constraint

LN_EPS = 1e-06
BF = jnp.bfloat16
F32 = jnp.float32
HI = lax.Precision.HIGHEST


def dot32(a, b, dims=((1,), (0,)), precision=None):
    return lax.dot_general(
        a, b, (dims, ((), ())), preferred_element_type=F32, precision=precision
    )


def swap(value, axis, bit):
    n = lax.axis_size(axis)
    return lax.ppermute(value, axis, [(i, i ^ bit) for i in range(n)])


def exchange(value):
    return lax.all_to_all(value, "expert", split_axis=0, concat_axis=0, tiled=True)


def line_steps(value, axis):
    n = lax.axis_size(axis)
    up, down = {}, {}
    cur_u = cur_d = value
    for s in range(1, n):
        cur_u = lax.ppermute(cur_u, axis, [(i, i + 1) for i in range(s - 1, n - 1)])
        cur_d = lax.ppermute(cur_d, axis, [(i, i - 1) for i in range(1, n - s + 1)])
        up[s], down[s] = cur_u, cur_d
    return up, down


def line_block(up, down, index, n, j):
    found = {}
    for i in range(n):
        found.setdefault((i ^ j) - i, []).append(i)
    total = None
    for gap, places in found.items():
        piece = down[gap] if gap > 0 else up[-gap]
        if total is None:
            total = piece
            continue
        here = functools.reduce(jnp.logical_or, [index == i for i in places])
        total = jnp.where(here, piece, total)
    return total


def chunk_of(size):
    for chunk in (256, 128):
        if size % chunk == 0:
            return chunk
    return size


def ffn_kernel(x_ref, c_ref, sel_ref, wr_ref, w1_ref, w2_ref, out_ref, back_ref, gh_ref, dp_ref, s_ref, gate, acc_o, acc_b, acc_s):
    step = pl.program_id(1)
    x = x_ref[...].reshape(c_ref.shape[1:])
    c = c_ref[0]

    @pl.when(step == 0)
    def _():
        logits = dot32(x, wr_ref[...])
        gate[...] = jax.nn.sigmoid(jnp.sum(logits * sel_ref[0], axis=1, keepdims=True))
        acc_o[...] = jnp.zeros_like(acc_o)
        acc_b[...] = jnp.zeros_like(acc_b)
        acc_s[...] = jnp.zeros_like(acc_s)

    g = gate[...]
    w1 = w1_ref[0]
    w2 = w2_ref[0]
    pre = dot32(x, w1)
    cdf = 0.5 * (1.0 + lax.erf(pre * 0.7071067811865476))
    hid = pre * cdf
    slope = cdf + pre * jnp.exp(-0.5 * pre * pre) * 0.3989422804014327
    hid_bf = hid.astype(BF)
    acc_o[...] += dot32(hid_bf, w2)
    dh = dot32(c, w2, ((1,), (1,))) * g
    dp = (dh * slope).astype(BF)
    acc_b[...] += dot32(dp, w1, ((1,), (1,)))
    acc_s[...] += jnp.sum(dh * hid, axis=1, keepdims=True)
    gh_ref[0] = (hid * g).astype(BF)
    dp_ref[0] = dp

    @pl.when(step == pl.num_programs(1) - 1)
    def _():
        out_ref[...] = (acc_o[...] * g).astype(BF).reshape(out_ref.shape)
        back_ref[...] = acc_b[...].astype(BF).reshape(back_ref.shape)
        s_ref[0] = acc_s[...]


def ffn(x, c, sel, w_router, w1, w2):
    e, rows, width = c.shape
    sources, seg = x.shape[0], x.shape[2]
    hidden = w1.shape[2]
    experts = w_router.shape[1]
    hc = chunk_of(hidden)
    row_spec = pl.BlockSpec((1, rows, width), lambda i, j: (i, 0, 0))
    src_spec = pl.BlockSpec((sources, None, seg, width), lambda i, j: (0, i, 0, 0))
    hid_spec = pl.BlockSpec((1, rows, hc), lambda i, j: (i, 0, j))
    return pl.pallas_call(
        ffn_kernel,
        grid=(e, hidden // hc),
        in_specs=[
            src_spec,
            row_spec,
            pl.BlockSpec((1, rows, experts), lambda i, j: (i, 0, 0)),
            pl.BlockSpec((width, experts), lambda i, j: (0, 0)),
            pl.BlockSpec((1, width, hc), lambda i, j: (i, 0, j)),
            pl.BlockSpec((1, hc, width), lambda i, j: (i, j, 0)),
        ],
        out_specs=[src_spec, src_spec, hid_spec, hid_spec, pl.BlockSpec((1, rows, 1), lambda i, j: (i, 0, 0))],
        out_shape=[
            jax.ShapeDtypeStruct(x.shape, BF),
            jax.ShapeDtypeStruct(x.shape, BF),
            jax.ShapeDtypeStruct((e, rows, hidden), BF),
            jax.ShapeDtypeStruct((e, rows, hidden), BF),
            jax.ShapeDtypeStruct((e, rows, 1), F32),
        ],
        scratch_shapes=[
            pltpu.VMEM((rows, 1), F32),
            pltpu.VMEM((rows, width), F32),
            pltpu.VMEM((rows, width), F32),
            pltpu.VMEM((rows, 1), F32),
        ],
        cost_estimate=pl.CostEstimate(
            flops=8 * e * rows * width * hidden,
            bytes_accessed=4 * e * width * hidden + 8 * e * rows * (width + hidden),
            transcendentals=2 * e * rows * hidden,
        ),
        compiler_params=pltpu.CompilerParams(dimension_semantics=("arbitrary", "arbitrary")),
    )(x, c, sel, w_router, w1, w2)


def wgrad_kernel(scale, pairs, *refs):
    total = None
    for i in range(pairs):
        left, right = [r[...].reshape(-1, r.shape[-1]) for r in (refs[i], refs[pairs + i])]
        term = dot32(left, right, ((0,), (0,)))
        total = term if total is None else total + term
    refs[-1][0] = total * scale


def wgrad(scale, lefts, rights):
    m = lefts[0].shape[-1]
    e, _, n = [a for a in rights + lefts if a.ndim == 3][0].shape
    n = rights[0].shape[-1]
    mc = chunk_of(m)
    rows = sum([a.size // (e * m) for a in lefts])

    def spec(a, size, step):
        if a.ndim == 3:
            return pl.BlockSpec((None, a.shape[1], size), lambda i, j: (i, 0, j * step))
        return pl.BlockSpec((a.shape[0], None, a.shape[2], size), lambda i, j: (0, i, 0, j * step))

    return pl.pallas_call(
        functools.partial(wgrad_kernel, scale, len(lefts)),
        grid=(e, m // mc),
        in_specs=[spec(a, mc, 1) for a in lefts] + [spec(b, n, 0) for b in rights],
        out_specs=pl.BlockSpec((1, mc, n), lambda i, j: (i, j, 0)),
        out_shape=jax.ShapeDtypeStruct((e, m, n), F32),
        cost_estimate=pl.CostEstimate(
            flops=2 * e * rows * m * n,
            bytes_accessed=4 * e * m * n + 2 * e * rows * (m + n),
            transcendentals=0,
        ),
        compiler_params=pltpu.CompilerParams(dimension_semantics=("arbitrary", "arbitrary")),
    )(*lefts, *rights)


def on_device(residual, context, w_out, w_router, expert_ids, w_fc1, w_fc2, cotangent):
    tok, width = residual.shape
    top_k = expert_ids.shape[1]
    n_dp = lax.axis_size("dp")
    n_ex = lax.axis_size("expert")
    z = lax.axis_index("dp")
    ex = lax.axis_index("expert")
    exp_dev = w_fc1.shape[0]
    experts = exp_dev * n_ex
    cap = max(2, (5 * top_k * tok + 4 * experts - 1) // (4 * experts))
    scale = float(tok * n_dp * n_ex) ** (-0.5)
    shard = w_out.shape[0]
    rows_q = n_dp * shard
    hi, lo = n_ex // 2, n_ex // 4
    groups = [list(range(n_dp // 2)), list(range(n_dp // 2, n_dp))]
    per = n_dp // 2
    seg = per * cap
    slots = n_ex * exp_dev * seg

    own_ids = expert_ids.T
    ids = [own_ids] + [swap(own_ids, "dp", j) for j in range(1, n_dp)]

    col = lax.broadcasted_iota(jnp.int32, (1, width), 1)
    place = col // rows_q
    within = col % rows_q
    rel = jnp.zeros_like(place)
    b, m = 1, n_ex // 2
    while m:
        rel = rel + ((place // m) % 2) * b
        b, m = b * 2, m // 2
    source = ((z ^ (within // shard)) * n_ex + (ex ^ rel)) * shard + within % shard
    reorder = (lax.broadcasted_iota(jnp.int32, (width, width), 0) == source).astype(BF)
    ctx_rel = dot32(context, reorder).astype(BF)

    tri = (
        lax.broadcasted_iota(jnp.int32, (tok, tok), 0)
        < lax.broadcasted_iota(jnp.int32, (tok, tok), 1)
    ).astype(BF)
    e_iota = lax.broadcasted_iota(jnp.int32, (experts, tok), 0)

    def spots_of(block):
        hot = [(e_iota == block[k : k + 1]).astype(F32) for k in range(top_k)]
        before = dot32(sum(hot).astype(BF), tri)
        return [jnp.sum(h * before, axis=0, keepdims=True).astype(jnp.int32) for h in hot]

    own_spots = spots_of(own_ids)
    spot_iota = lax.broadcasted_iota(jnp.int32, (experts * cap, 1), 0)
    own_map = sum([(spot_iota == own_ids[k : k + 1] * cap + own_spots[k]).astype(BF) for k in range(top_k)])
    own_sent = dot32(own_map, cotangent).astype(BF)
    own_cot = exchange(own_sent)

    ids = lax.optimization_barrier(ids)
    spots = [spots_of(block) for block in ids]
    slot_iota = lax.broadcasted_iota(jnp.int32, (slots, 1), 0)
    maps = []
    for group in groups:
        by_k = []
        for k in range(top_k):
            target = [
                (ids[j][k : k + 1] // exp_dev) * (exp_dev * seg)
                + (ids[j][k : k + 1] % exp_dev) * seg
                + i * cap
                + spots[j][k]
                for i, j in enumerate(group)
            ]
            by_k.append((slot_iota == jnp.concatenate(target, axis=1)).astype(BF))
        maps.append(by_k)
    merged = [m[0] + m[1] for m in maps]

    def spread(value):
        n = value.shape[1]
        padded = -(-n // 1024) * 1024
        tile = jnp.pad(value, ((0, 0), (0, padded - n))).reshape(-1, 128)
        got = exchange(tile)
        return got.reshape(n_ex, padded)[:, :n]

    others = []
    for group, by_k in zip(groups, maps):
        total = None
        for k in range(top_k):
            value = jnp.concatenate([ids[j][1 - k : 2 - k] for j in group], axis=1).astype(BF)
            term = dot32(value, by_k[k], ((1,), (1,)))
            total = term if total is None else total + term
        others.append(total.reshape(n_ex, exp_dev * seg))
    others = spread(jnp.concatenate(others, axis=1))
    rows = n_ex * seg
    sels = []
    own_expert = ex * exp_dev + lax.broadcasted_iota(jnp.int32, (exp_dev, 1, 1), 0)
    lane_expert = lax.broadcasted_iota(jnp.int32, (1, 1, experts), 2)
    for g in range(len(groups)):
        other = others[:, g * exp_dev * seg : (g + 1) * exp_dev * seg]
        other = other.reshape(n_ex, exp_dev, seg).transpose(1, 0, 2).reshape(exp_dev, rows, 1)
        sels.append(
            (lane_expert == own_expert).astype(F32)
            - (lane_expert == other.astype(jnp.int32)).astype(F32)
        )

    def dispatch(blocks, hot):
        sent = dot32(hot, jnp.concatenate(blocks, axis=0)).astype(BF)
        return exchange(sent).reshape(n_ex, exp_dev, seg, width)

    w_dp = jnp.concatenate([w_out] + [swap(w_out, "dp", j) for j in range(1, n_dp)], axis=0)
    from_hi = swap(w_dp, "expert", hi)
    from_lo = swap(w_dp, "expert", lo)
    half_q = rows_q // 2
    diag_a = swap(from_hi[:half_q], "expert", lo)
    diag_b = swap(from_lo[half_q:], "expert", hi)
    w_rel = [jnp.concatenate([w_dp, from_hi, from_lo, diag_a, diag_b], axis=0)]
    bit = lo // 2
    while bit:
        w_rel = w_rel + [swap(piece, "expert", bit) for piece in w_rel]
        bit //= 2

    stream = residual.astype(F32)
    span = w_rel[0].shape[0]
    for i, piece in enumerate(w_rel):
        stream = stream + dot32(ctx_rel[:, i * span : (i + 1) * span], piece)
    average = jnp.mean(stream, axis=1, keepdims=True)
    centred = stream - average
    variance = jnp.mean(centred * centred, axis=1, keepdims=True)
    inv_std = lax.rsqrt(variance + LN_EPS)
    normed = centred * inv_std
    normed_bf = normed.astype(BF)
    xs = [normed_bf] + [swap(normed_bf, "dp", j) for j in range(1, n_dp)]
    slot_in = [dispatch([xs[j] for j in group], hot) for group, hot in zip(groups, merged)]

    up, down = line_steps(own_cot, "dp")
    cots = [own_cot] + [line_block(up, down, z, n_dp, j) for j in range(1, n_dp)]
    line = exp_dev * rows
    at = lax.broadcasted_iota(jnp.int32, (line, 1), 0)
    e_at, src_at, blk_at, pos_at = at // rows, at % rows // seg, at % seg // cap, at % cap
    came_from = ((blk_at * n_ex + src_at) * exp_dev + e_at) * cap + pos_at
    arrange = (came_from == lax.broadcasted_iota(jnp.int32, (line, line), 1)).astype(BF)
    slot_cot = [
        dot32(arrange, jnp.concatenate([cots[j] for j in group], axis=0)).astype(BF).reshape(exp_dev, rows, width)
        for group in groups
    ]

    logits = dot32(w_router, normed_bf, ((0,), (1,)))
    late_ids = lax.optimization_barrier(own_ids)
    picks = [(e_iota == late_ids[k : k + 1]).astype(F32) for k in range(top_k)]
    chosen = jnp.concatenate([jnp.sum(h * logits, axis=0, keepdims=True) for h in picks], axis=0)
    gates = jax.nn.sigmoid(chosen - chosen[::-1])

    results = []
    for x, c, sel in zip(slot_in, slot_cot, sels):
        results.append(ffn(x, c, sel, w_router, w_fc1, w_fc2))

    def collect(value, hot):
        got = exchange(value.reshape(-1, width))
        return dot32(hot, got, ((0,), (0,)))

    def reduce_dp(parts):
        total = parts[0]
        for j in range(1, n_dp):
            total = total + swap(parts[j].astype(BF), "dp", j).astype(F32)
        return total

    def blocks_of(values):
        return [v[i * tok : (i + 1) * tok] for v in values for i in range(per)]

    back_sum = reduce_dp(blocks_of([collect(r[1], hot) for r, hot in zip(results, merged)]))
    score = [
        r[4].reshape(exp_dev, n_ex, seg).transpose(1, 0, 2).reshape(n_ex, exp_dev * seg)
        for r in results
    ]
    score = spread(jnp.concatenate(score, axis=1))
    part = exp_dev * seg
    score_parts = []
    for g, by_k in enumerate(maps):
        line = score[:, g * part : (g + 1) * part].reshape(1, slots)
        both = jnp.concatenate([dot32(line, by_k[k].astype(F32), precision=HI) for k in range(top_k)], axis=0)
        score_parts += [both[:, i * tok : (i + 1) * tok] for i in range(per)]
    score_sum = score_parts[0]
    for j in range(1, n_dp):
        score_sum = score_sum + swap(score_parts[j], "dp", j)
    mixture = reduce_dp(blocks_of([collect(r[0], hot) for r, hot in zip(results, merged)]))
    d_chosen = score_sum - gates * jnp.sum(score_sum, axis=0, keepdims=True)
    d_logits = sum([picks[k] * d_chosen[k : k + 1] for k in range(top_k)])
    d_normed = back_sum + dot32(d_logits, w_router.astype(F32), ((0,), (1,)), precision=HI)
    cot_float = cotangent.astype(F32)
    d_stream = cot_float + inv_std * (
        d_normed
        - jnp.mean(d_normed, axis=1, keepdims=True)
        - normed * jnp.mean(d_normed * normed, axis=1, keepdims=True)
    )
    d_residual, late_stream = lax.optimization_barrier((d_stream.astype(BF), stream))
    layer_out = (late_stream + mixture).astype(BF)
    d_rel = jnp.concatenate([dot32(d_residual, piece, ((1,), (1,))).astype(BF) for piece in w_rel], axis=1)
    d_context = dot32(d_rel, reorder, ((1,), (1,))).astype(BF)

    router_term = dot32(normed_bf.astype(F32), d_logits, ((0,), (1,)), precision=HI)
    router_term = dot32(reorder.astype(F32), router_term, ((0,), (0,)), precision=HI)
    pad = -experts % 128
    part_out = jnp.concatenate(
        [dot32(ctx_rel, d_residual, ((0,), (0,))), jnp.pad(router_term, ((0, 0), (0, pad)))], axis=1
    )
    part_out = with_layout_constraint(part_out, Layout(major_to_minor=(0, 1)))
    bit = 1
    while bit < lo:
        half = part_out.shape[0] // 2
        part_out = part_out[:half] + swap(part_out[half:].astype(BF), "expert", bit).astype(F32)
        bit *= 2
    mid = width // 2
    quarters = [part_out[i * rows_q : (i + 1) * rows_q] for i in range(4)]
    left = [q[:, :mid] for q in quarters]
    right = [q[:, mid:] for q in quarters]
    got_l = swap(jnp.concatenate([left[2], left[3]], axis=0).astype(BF), "expert", lo).astype(F32)
    got_r = swap(jnp.concatenate([right[1], right[3]], axis=0).astype(BF), "expert", hi).astype(F32)
    fin_l = swap((left[1] + got_l[rows_q:]).astype(BF), "expert", hi).astype(F32)
    fin_r = swap((right[2] + got_r[rows_q:]).astype(BF), "expert", lo).astype(F32)
    kept = jnp.concatenate([left[0] + got_l[:rows_q] + fin_l, right[0] + got_r[:rows_q] + fin_r], axis=1)
    grads = kept[:shard]
    for j in range(1, n_dp):
        grads = grads + swap(kept[j * shard : (j + 1) * shard].astype(BF), "dp", j).astype(F32)
    grad_out = scale * grads[:, :width]
    grad_router = scale * grads[:, width : width + experts]

    grad_fc1 = wgrad(scale, slot_in, [r[3] for r in results])
    grad_fc2 = wgrad(scale, [r[2] for r in results], slot_cot)
    return (layer_out, d_residual, d_context, grad_out, grad_router, grad_fc1, grad_fc2)


def solution(mesh):
    rows = P(("dp", "expert"), None)
    first = P("expert", None, "dp")
    second = P("expert", "dp", None)

    return jax.shard_map(
        on_device,
        mesh=mesh,
        in_specs=(rows, rows, rows, P(), rows, first, second, rows),
        out_specs=(rows, rows, rows, rows, rows, first, second),
        check_vma=False,
    )
```

```python
import functools

import jax
import jax.numpy as jnp
from jax import lax
from jax.experimental import pallas as pl
from jax.experimental.pallas import tpu as pltpu
from jax.sharding import PartitionSpec as P

from jax.experimental.layout import Layout, with_layout_constraint

LN_EPS = 1e-06
BF = jnp.bfloat16
F32 = jnp.float32
HI = lax.Precision.HIGHEST


def dot32(a, b, dims=((1,), (0,)), precision=None):
    return lax.dot_general(
        a, b, (dims, ((), ())), preferred_element_type=F32, precision=precision
    )


def swap(value, axis, bit):
    n = lax.axis_size(axis)
    return lax.ppermute(value, axis, [(i, i ^ bit) for i in range(n)])


def exchange(value):
    return lax.all_to_all(value, "expert", split_axis=0, concat_axis=0, tiled=True)


def chunk_of(size):
    for chunk in (256, 128):
        if size % chunk == 0:
            return chunk
    return size


def flat(ref):
    return ref[...].reshape(-1, ref.shape[-1])


def row_block(a, size, step):
    if a.ndim == 3:
        return pl.BlockSpec((None, a.shape[1], size), lambda i, j: (i, 0, j * step))
    return pl.BlockSpec((a.shape[0], None, a.shape[2], size), lambda i, j: (0, i, 0, j * step))


def ffn_kernel(x_ref, c_ref, sel_ref, wr_ref, w1_ref, w2_ref, out_ref, back_ref, gh_ref, dp_ref, s_ref, gate, acc_o, acc_b, acc_s):
    step = pl.program_id(1)
    x = flat(x_ref)
    c = flat(c_ref)

    @pl.when(step == 0)
    def _():
        logits = dot32(x, wr_ref[...])
        gate[...] = jax.nn.sigmoid(jnp.sum(logits * sel_ref[0], axis=1, keepdims=True))
        acc_o[...] = jnp.zeros_like(acc_o)
        acc_b[...] = jnp.zeros_like(acc_b)
        acc_s[...] = jnp.zeros_like(acc_s)

    g = gate[...]
    w1 = w1_ref[0]
    w2 = w2_ref[0]
    pre = dot32(x, w1)
    cdf = 0.5 * (1.0 + lax.erf(pre * 0.7071067811865476))
    hid = pre * cdf
    slope = cdf + pre * jnp.exp(-0.5 * pre * pre) * 0.3989422804014327
    hid_bf = hid.astype(BF)
    acc_o[...] += dot32(hid_bf, w2)
    dh = dot32(c, w2, ((1,), (1,))) * g
    dp = (dh * slope).astype(BF)
    acc_b[...] += dot32(dp, w1, ((1,), (1,)))
    acc_s[...] += jnp.sum(dh * hid, axis=1, keepdims=True)
    gh_ref[0] = (hid * g).astype(BF)
    dp_ref[0] = dp

    @pl.when(step == pl.num_programs(1) - 1)
    def _():
        out_ref[...] = (acc_o[...] * g).astype(BF).reshape(out_ref.shape)
        back_ref[...] = acc_b[...].astype(BF).reshape(back_ref.shape)
        s_ref[0] = acc_s[...]


def ffn(x, c, sel, w_router, w1, w2):
    e, width, hidden = w1.shape
    rows = x.size // (e * width)
    experts = w_router.shape[1]
    hc = chunk_of(hidden)
    row_spec = row_block(x, width, 0)
    hid_spec = pl.BlockSpec((1, rows, hc), lambda i, j: (i, 0, j))
    return pl.pallas_call(
        ffn_kernel,
        grid=(e, hidden // hc),
        in_specs=[
            row_spec,
            row_spec,
            pl.BlockSpec((1, rows, experts), lambda i, j: (i, 0, 0)),
            pl.BlockSpec((width, experts), lambda i, j: (0, 0)),
            pl.BlockSpec((1, width, hc), lambda i, j: (i, 0, j)),
            pl.BlockSpec((1, hc, width), lambda i, j: (i, j, 0)),
        ],
        out_specs=[row_spec, row_spec, hid_spec, hid_spec, pl.BlockSpec((1, rows, 1), lambda i, j: (i, 0, 0))],
        out_shape=[
            jax.ShapeDtypeStruct(x.shape, BF),
            jax.ShapeDtypeStruct(x.shape, BF),
            jax.ShapeDtypeStruct((e, rows, hidden), BF),
            jax.ShapeDtypeStruct((e, rows, hidden), BF),
            jax.ShapeDtypeStruct((e, rows, 1), F32),
        ],
        scratch_shapes=[
            pltpu.VMEM((rows, 1), F32),
            pltpu.VMEM((rows, width), F32),
            pltpu.VMEM((rows, width), F32),
            pltpu.VMEM((rows, 1), F32),
        ],
        cost_estimate=pl.CostEstimate(
            flops=8 * e * rows * width * hidden,
            bytes_accessed=4 * e * width * hidden + 8 * e * rows * (width + hidden),
            transcendentals=2 * e * rows * hidden,
        ),
        compiler_params=pltpu.CompilerParams(dimension_semantics=("arbitrary", "arbitrary")),
    )(x, c, sel, w_router, w1, w2)


def wgrad_kernel(scale, pairs, *refs):
    total = None
    for i in range(pairs):
        term = dot32(flat(refs[i]), flat(refs[pairs + i]), ((0,), (0,)))
        total = term if total is None else total + term
    refs[-1][0] = total * scale


def wgrad(scale, e, lefts, rights):
    m = lefts[0].shape[-1]
    n = rights[0].shape[-1]
    mc = chunk_of(m)
    rows = sum([a.size // (e * m) for a in lefts])
    return pl.pallas_call(
        functools.partial(wgrad_kernel, scale, len(lefts)),
        grid=(e, m // mc),
        in_specs=[row_block(a, mc, 1) for a in lefts] + [row_block(b, n, 0) for b in rights],
        out_specs=pl.BlockSpec((1, mc, n), lambda i, j: (i, j, 0)),
        out_shape=jax.ShapeDtypeStruct((e, m, n), F32),
        cost_estimate=pl.CostEstimate(
            flops=2 * e * rows * m * n,
            bytes_accessed=4 * e * m * n + 2 * e * rows * (m + n),
            transcendentals=0,
        ),
        compiler_params=pltpu.CompilerParams(dimension_semantics=("arbitrary", "arbitrary")),
    )(*lefts, *rights)


def on_device(residual, context, w_out, w_router, expert_ids, w_fc1, w_fc2, cotangent):
    tok, width = residual.shape
    top_k = expert_ids.shape[1]
    n_dp = lax.axis_size("dp")
    n_ex = lax.axis_size("expert")
    z = lax.axis_index("dp")
    ex = lax.axis_index("expert")
    exp_dev = w_fc1.shape[0]
    experts = exp_dev * n_ex
    cap = max(2, (5 * top_k * tok + 4 * experts - 1) // (4 * experts))
    scale = float(tok * n_dp * n_ex) ** (-0.5)
    shard = w_out.shape[0]
    rows_q = n_dp * shard
    hi, lo = n_ex // 2, n_ex // 4
    groups = [list(range(n_dp // 2)), list(range(n_dp // 2, n_dp))]
    per = n_dp // 2
    seg = per * cap
    slots = n_ex * exp_dev * seg

    own_ids = expert_ids.T
    ids = [own_ids] + [swap(own_ids, "dp", j) for j in range(1, n_dp)]

    col = lax.broadcasted_iota(jnp.int32, (1, width), 1)
    place = col // rows_q
    within = col % rows_q
    rel = jnp.zeros_like(place)
    b, m = 1, n_ex // 2
    while m:
        rel = rel + ((place // m) % 2) * b
        b, m = b * 2, m // 2
    source = ((z ^ (within // shard)) * n_ex + (ex ^ rel)) * shard + within % shard
    reorder = (lax.broadcasted_iota(jnp.int32, (width, width), 0) == source).astype(BF)
    ctx_rel = dot32(context, reorder).astype(BF)

    tri = (
        lax.broadcasted_iota(jnp.int32, (tok, tok), 0)
        < lax.broadcasted_iota(jnp.int32, (tok, tok), 1)
    ).astype(BF)
    e_iota = lax.broadcasted_iota(jnp.int32, (experts, tok), 0)

    def spots_of(block):
        hot = [(e_iota == block[k : k + 1]).astype(F32) for k in range(top_k)]
        before = dot32(sum(hot).astype(BF), tri)
        return [jnp.sum(h * before, axis=0, keepdims=True).astype(jnp.int32) for h in hot]

    own_spots = spots_of(own_ids)
    spot_iota = lax.broadcasted_iota(jnp.int32, (experts * cap, 1), 0)
    own_map = sum([(spot_iota == own_ids[k : k + 1] * cap + own_spots[k]).astype(BF) for k in range(top_k)])
    own_sent = dot32(own_map, cotangent).astype(BF)
    own_cot = exchange(own_sent)

    ids = lax.optimization_barrier(ids)
    spots = [spots_of(block) for block in ids]
    slot_iota = lax.broadcasted_iota(jnp.int32, (slots, 1), 0)
    maps = []
    for group in groups:
        by_k = []
        for k in range(top_k):
            target = [
                (ids[j][k : k + 1] // exp_dev) * (exp_dev * seg)
                + (ids[j][k : k + 1] % exp_dev) * seg
                + i * cap
                + spots[j][k]
                for i, j in enumerate(group)
            ]
            by_k.append((slot_iota == jnp.concatenate(target, axis=1)).astype(BF))
        maps.append(by_k)
    merged = [m[0] + m[1] for m in maps]

    def spread(value):
        n = value.shape[1]
        padded = -(-n // 1024) * 1024
        tile = jnp.pad(value, ((0, 0), (0, padded - n))).reshape(-1, 128)
        got = exchange(tile)
        return got.reshape(n_ex, padded)[:, :n]

    others = []
    for group, by_k in zip(groups, maps):
        total = None
        for k in range(top_k):
            value = jnp.concatenate([ids[j][1 - k : 2 - k] for j in group], axis=1).astype(BF)
            term = dot32(value, by_k[k], ((1,), (1,)))
            total = term if total is None else total + term
        others.append(total.reshape(n_ex, exp_dev * seg))
    others = spread(jnp.concatenate(others, axis=1))
    rows = n_ex * seg
    sels = []
    own_expert = ex * exp_dev + lax.broadcasted_iota(jnp.int32, (exp_dev, 1, 1), 0)
    lane_expert = lax.broadcasted_iota(jnp.int32, (1, 1, experts), 2)
    for g in range(len(groups)):
        other = others[:, g * exp_dev * seg : (g + 1) * exp_dev * seg]
        if g == 0:
            other = other.reshape(n_ex, exp_dev, per, cap).transpose(1, 2, 0, 3)
        else:
            other = other.reshape(n_ex, exp_dev, seg).transpose(1, 0, 2)
        other = other.reshape(exp_dev, rows, 1)
        sels.append(
            (lane_expert == own_expert).astype(F32)
            - (lane_expert == other.astype(jnp.int32)).astype(F32)
        )

    def dispatch(blocks, hot):
        sent = dot32(hot, jnp.concatenate(blocks, axis=0)).astype(BF)
        return exchange(sent).reshape(n_ex, exp_dev, seg, width)

    near, far = groups
    line = exp_dev * rows
    at = lax.broadcasted_iota(jnp.int32, (line, 1), 0)
    e_at, blk_at, src_at, pos_at = at // rows, at % rows // (n_ex * cap), at % (n_ex * cap) // cap, at % cap
    came_from = ((blk_at * n_ex + src_at) * exp_dev + e_at) * cap + pos_at
    arrange = (came_from == lax.broadcasted_iota(jnp.int32, (line, line), 1)).astype(BF)

    def gather_near(own):
        every = [own] + [swap(own, "dp", j) for j in near[1:]]
        return dot32(arrange, jnp.concatenate(every, axis=0)).astype(BF).reshape(exp_dev, rows, width)

    cot_near = gather_near(own_cot)
    cots = [swap(cotangent, "dp", j) for j in far]
    slot_cot = [cot_near, dispatch(cots, merged[1])]

    w_dp = jnp.concatenate([w_out] + [swap(w_out, "dp", j) for j in range(1, n_dp)], axis=0)
    from_hi = swap(w_dp, "expert", hi)
    from_lo = swap(w_dp, "expert", lo)
    half_q = rows_q // 2
    diag_a = swap(from_hi[:half_q], "expert", lo)
    diag_b = swap(from_lo[half_q:], "expert", hi)
    w_rel = [jnp.concatenate([w_dp, from_hi, from_lo, diag_a, diag_b], axis=0)]
    bit = lo // 2
    while bit:
        w_rel = w_rel + [swap(piece, "expert", bit) for piece in w_rel]
        bit //= 2

    stream = residual.astype(F32)
    span = w_rel[0].shape[0]
    for i, piece in enumerate(w_rel):
        stream = stream + dot32(ctx_rel[:, i * span : (i + 1) * span], piece)
    average = jnp.mean(stream, axis=1, keepdims=True)
    centred = stream - average
    variance = jnp.mean(centred * centred, axis=1, keepdims=True)
    inv_std = lax.rsqrt(variance + LN_EPS)
    normed = centred * inv_std
    normed_bf = normed.astype(BF)
    xs = [swap(normed_bf, "dp", j) for j in far]
    own_in = exchange(dot32(own_map, normed_bf).astype(BF))
    slot_in = [gather_near(own_in), dispatch(xs, merged[1])]

    logits = dot32(w_router, normed_bf, ((0,), (1,)))
    late_ids = lax.optimization_barrier(own_ids)
    picks = [(e_iota == late_ids[k : k + 1]).astype(F32) for k in range(top_k)]
    chosen = jnp.concatenate([jnp.sum(h * logits, axis=0, keepdims=True) for h in picks], axis=0)
    gates = jax.nn.sigmoid(chosen - chosen[::-1])

    results = []
    for x, c, sel in zip(slot_in, slot_cot, sels):
        results.append(ffn(x, c, sel, w_router, w_fc1, w_fc2))

    def collect(near_part, far_part):
        pieces = dot32(arrange, near_part.reshape(line, width), ((0,), (0,))).astype(BF)
        size = line // per
        slots_own = pieces[:size].astype(F32)
        for j in near[1:]:
            slots_own = slots_own + swap(pieces[j * size : (j + 1) * size], "dp", j).astype(F32)
        got = exchange(slots_own.astype(BF))
        total = dot32(own_map, got, ((0,), (0,)))
        got = exchange(far_part.reshape(-1, width))
        parts = dot32(merged[1], got, ((0,), (0,))).astype(BF)
        for i, j in enumerate(far):
            total = total + swap(parts[i * tok : (i + 1) * tok], "dp", j).astype(F32)
        return total

    back_sum = collect(results[0][1], results[1][1])
    score = [
        results[0][4].reshape(exp_dev, per, n_ex, cap).transpose(2, 0, 1, 3).reshape(n_ex, exp_dev * seg),
        results[1][4].reshape(exp_dev, n_ex, seg).transpose(1, 0, 2).reshape(n_ex, exp_dev * seg),
    ]
    score = spread(jnp.concatenate(score, axis=1))
    part = exp_dev * seg
    score_parts = []
    for g, by_k in enumerate(maps):
        packed = score[:, g * part : (g + 1) * part].reshape(1, slots)
        both = jnp.concatenate([dot32(packed, by_k[k].astype(F32), precision=HI) for k in range(top_k)], axis=0)
        score_parts += [both[:, i * tok : (i + 1) * tok] for i in range(per)]
    score_sum = score_parts[0]
    for j in range(1, n_dp):
        score_sum = score_sum + swap(score_parts[j], "dp", j)
    mixture = collect(results[0][0], results[1][0])
    d_chosen = score_sum - gates * jnp.sum(score_sum, axis=0, keepdims=True)
    d_logits = sum([picks[k] * d_chosen[k : k + 1] for k in range(top_k)])
    d_normed = back_sum + dot32(d_logits, w_router.astype(F32), ((0,), (1,)), precision=HI)
    cot_float = cotangent.astype(F32)
    d_stream = cot_float + inv_std * (
        d_normed
        - jnp.mean(d_normed, axis=1, keepdims=True)
        - normed * jnp.mean(d_normed * normed, axis=1, keepdims=True)
    )
    d_residual, late_stream = lax.optimization_barrier((d_stream.astype(BF), stream))
    layer_out = (late_stream + mixture).astype(BF)
    d_rel = jnp.concatenate([dot32(d_residual, piece, ((1,), (1,))).astype(BF) for piece in w_rel], axis=1)
    d_context = dot32(d_rel, reorder, ((1,), (1,))).astype(BF)

    router_term = dot32(normed_bf.astype(F32), d_logits, ((0,), (1,)), precision=HI)
    router_term = dot32(reorder.astype(F32), router_term, ((0,), (0,)), precision=HI)
    pad = -experts % 128
    part_out = jnp.concatenate(
        [dot32(ctx_rel, d_residual, ((0,), (0,))), jnp.pad(router_term, ((0, 0), (0, pad)))], axis=1
    )
    part_out = with_layout_constraint(part_out, Layout(major_to_minor=(0, 1)))
    bit = 1
    while bit < lo:
        half = part_out.shape[0] // 2
        part_out = part_out[:half] + swap(part_out[half:].astype(BF), "expert", bit).astype(F32)
        bit *= 2
    mid = width // 2
    quarters = [part_out[i * rows_q : (i + 1) * rows_q] for i in range(4)]
    left = [q[:, :mid] for q in quarters]
    right = [q[:, mid:] for q in quarters]
    got_l = swap(jnp.concatenate([left[2], left[3]], axis=0).astype(BF), "expert", lo).astype(F32)
    got_r = swap(jnp.concatenate([right[1], right[3]], axis=0).astype(BF), "expert", hi).astype(F32)
    fin_l = swap((left[1] + got_l[rows_q:]).astype(BF), "expert", hi).astype(F32)
    fin_r = swap((right[2] + got_r[rows_q:]).astype(BF), "expert", lo).astype(F32)
    kept = jnp.concatenate([left[0] + got_l[:rows_q] + fin_l, right[0] + got_r[:rows_q] + fin_r], axis=1)
    grads = kept[:shard]
    for j in range(1, n_dp):
        grads = grads + swap(kept[j * shard : (j + 1) * shard].astype(BF), "dp", j).astype(F32)
    grad_out = scale * grads[:, :width]
    grad_router = scale * grads[:, width : width + experts]

    grad_fc1 = wgrad(scale, exp_dev, slot_in, [r[3] for r in results])
    grad_fc2 = wgrad(scale, exp_dev, [r[2] for r in results], slot_cot)
    return (layer_out, d_residual, d_context, grad_out, grad_router, grad_fc1, grad_fc2)


def solution(mesh):
    rows = P(("dp", "expert"), None)
    first = P("expert", None, "dp")
    second = P("expert", "dp", None)

    return jax.shard_map(
        on_device,
        mesh=mesh,
        in_specs=(rows, rows, rows, P(), rows, first, second, rows),
        out_specs=(rows, rows, rows, rows, rows, first, second),
        check_vma=False,
    )
```

```python
import functools

import jax
import jax.numpy as jnp
from jax import lax
from jax.experimental import pallas as pl
from jax.experimental.pallas import tpu as pltpu
from jax.sharding import PartitionSpec as P

LN_EPS = 1e-06
BF = jnp.bfloat16
F32 = jnp.float32
HI = lax.Precision.HIGHEST


def dot32(a, b, dims=((1,), (0,)), precision=None):
    return lax.dot_general(
        a, b, (dims, ((), ())), preferred_element_type=F32, precision=precision
    )


def swap(value, axis, bit):
    n = lax.axis_size(axis)
    return lax.ppermute(value, axis, [(i, i ^ bit) for i in range(n)])


def exchange(value):
    return lax.all_to_all(value, "expert", split_axis=0, concat_axis=0, tiled=True)


def chunk_of(size):
    for chunk in (256, 128):
        if size % chunk == 0:
            return chunk
    return size


def flat(ref):
    return ref[...].reshape(-1, ref.shape[-1])


def row_block(a, size, step):
    if a.ndim == 3:
        return pl.BlockSpec((None, a.shape[1], size), lambda i, j: (i, 0, j * step))
    return pl.BlockSpec((a.shape[0], None, a.shape[2], size), lambda i, j: (0, i, 0, j * step))


def ffn_kernel(x_ref, c_ref, sel_ref, wr_ref, w1_ref, w2_ref, out_ref, back_ref, gh_ref, dp_ref, s_ref, gate, acc_o, acc_b, acc_s):
    step = pl.program_id(1)
    x = flat(x_ref)
    c = flat(c_ref)

    @pl.when(step == 0)
    def _():
        logits = dot32(x, wr_ref[...])
        gate[...] = jax.nn.sigmoid(jnp.sum(logits * sel_ref[0], axis=1, keepdims=True))
        acc_o[...] = jnp.zeros_like(acc_o)
        acc_b[...] = jnp.zeros_like(acc_b)
        acc_s[...] = jnp.zeros_like(acc_s)

    g = gate[...]
    w1 = w1_ref[0]
    w2 = w2_ref[0]
    pre = dot32(x, w1)
    cdf = 0.5 * (1.0 + lax.erf(pre * 0.7071067811865476))
    hid = pre * cdf
    slope = cdf + pre * jnp.exp(-0.5 * pre * pre) * 0.3989422804014327
    hid_bf = hid.astype(BF)
    acc_o[...] += dot32(hid_bf, w2)
    dh = dot32(c, w2, ((1,), (1,))) * g
    dp = (dh * slope).astype(BF)
    acc_b[...] += dot32(dp, w1, ((1,), (1,)))
    acc_s[...] += jnp.sum(dh * hid, axis=1, keepdims=True)
    gh_ref[0] = (hid * g).astype(BF)
    dp_ref[0] = dp

    @pl.when(step == pl.num_programs(1) - 1)
    def _():
        out_ref[...] = (acc_o[...] * g).astype(BF).reshape(out_ref.shape)
        back_ref[...] = acc_b[...].astype(BF).reshape(back_ref.shape)
        s_ref[0] = acc_s[...]


def ffn(x, c, sel, w_router, w1, w2):
    e, width, hidden = w1.shape
    rows = x.size // (e * width)
    experts = w_router.shape[1]
    hc = chunk_of(hidden)
    row_spec = row_block(x, width, 0)
    hid_spec = pl.BlockSpec((1, rows, hc), lambda i, j: (i, 0, j))
    return pl.pallas_call(
        ffn_kernel,
        grid=(e, hidden // hc),
        in_specs=[
            row_spec,
            row_spec,
            pl.BlockSpec((1, rows, experts), lambda i, j: (i, 0, 0)),
            pl.BlockSpec((width, experts), lambda i, j: (0, 0)),
            pl.BlockSpec((1, width, hc), lambda i, j: (i, 0, j)),
            pl.BlockSpec((1, hc, width), lambda i, j: (i, j, 0)),
        ],
        out_specs=[row_spec, row_spec, hid_spec, hid_spec, pl.BlockSpec((1, rows, 1), lambda i, j: (i, 0, 0))],
        out_shape=[
            jax.ShapeDtypeStruct(x.shape, BF),
            jax.ShapeDtypeStruct(x.shape, BF),
            jax.ShapeDtypeStruct((e, rows, hidden), BF),
            jax.ShapeDtypeStruct((e, rows, hidden), BF),
            jax.ShapeDtypeStruct((e, rows, 1), F32),
        ],
        scratch_shapes=[
            pltpu.VMEM((rows, 1), F32),
            pltpu.VMEM((rows, width), F32),
            pltpu.VMEM((rows, width), F32),
            pltpu.VMEM((rows, 1), F32),
        ],
        cost_estimate=pl.CostEstimate(
            flops=8 * e * rows * width * hidden,
            bytes_accessed=4 * e * width * hidden + 8 * e * rows * (width + hidden),
            transcendentals=2 * e * rows * hidden,
        ),
        compiler_params=pltpu.CompilerParams(dimension_semantics=("arbitrary", "arbitrary")),
    )(x, c, sel, w_router, w1, w2)


def wgrad_kernel(scale, pairs, *refs):
    total = None
    for i in range(pairs):
        term = dot32(flat(refs[i]), flat(refs[pairs + i]), ((0,), (0,)))
        total = term if total is None else total + term
    refs[-1][0] = total * scale


def wgrad(scale, e, lefts, rights):
    m = lefts[0].shape[-1]
    n = rights[0].shape[-1]
    mc = chunk_of(m)
    rows = sum([a.size // (e * m) for a in lefts])
    return pl.pallas_call(
        functools.partial(wgrad_kernel, scale, len(lefts)),
        grid=(e, m // mc),
        in_specs=[row_block(a, mc, 1) for a in lefts] + [row_block(b, n, 0) for b in rights],
        out_specs=pl.BlockSpec((1, mc, n), lambda i, j: (i, j, 0)),
        out_shape=jax.ShapeDtypeStruct((e, m, n), F32),
        cost_estimate=pl.CostEstimate(
            flops=2 * e * rows * m * n,
            bytes_accessed=4 * e * m * n + 2 * e * rows * (m + n),
            transcendentals=0,
        ),
        compiler_params=pltpu.CompilerParams(dimension_semantics=("arbitrary", "arbitrary")),
    )(*lefts, *rights)


def on_device(residual, context, w_out, w_router, expert_ids, w_fc1, w_fc2, cotangent):
    tok, width = residual.shape
    top_k = expert_ids.shape[1]
    n_dp = lax.axis_size("dp")
    n_ex = lax.axis_size("expert")
    z = lax.axis_index("dp")
    ex = lax.axis_index("expert")
    exp_dev = w_fc1.shape[0]
    experts = exp_dev * n_ex
    cap = max(2, (5 * top_k * tok + 4 * experts - 1) // (4 * experts))
    scale = float(tok * n_dp * n_ex) ** (-0.5)
    shard = w_out.shape[0]
    rows_q = n_dp * shard
    hi, lo = n_ex // 2, n_ex // 4
    groups = [list(range(n_dp // 2)), list(range(n_dp // 2, n_dp))]
    per = n_dp // 2
    seg = per * cap
    slots = n_ex * exp_dev * seg

    own_ids = expert_ids.T
    ids = [own_ids] + [swap(own_ids, "dp", j) for j in range(1, n_dp)]

    col = lax.broadcasted_iota(jnp.int32, (1, width), 1)
    place = col // rows_q
    within = col % rows_q
    rel = jnp.zeros_like(place)
    b, m = 1, n_ex // 2
    while m:
        rel = rel + ((place // m) % 2) * b
        b, m = b * 2, m // 2
    source = ((z ^ (within // shard)) * n_ex + (ex ^ rel)) * shard + within % shard
    reorder = (lax.broadcasted_iota(jnp.int32, (width, width), 0) == source).astype(BF)
    ctx_rel = dot32(context, reorder).astype(BF)

    tri = (
        lax.broadcasted_iota(jnp.int32, (tok, tok), 0)
        < lax.broadcasted_iota(jnp.int32, (tok, tok), 1)
    ).astype(BF)
    e_iota = lax.broadcasted_iota(jnp.int32, (experts, tok), 0)

    def spots_of(block):
        hot = [(e_iota == block[k : k + 1]).astype(F32) for k in range(top_k)]
        before = dot32(sum(hot).astype(BF), tri)
        return [jnp.sum(h * before, axis=0, keepdims=True).astype(jnp.int32) for h in hot]

    own_spots = spots_of(own_ids)
    spot_iota = lax.broadcasted_iota(jnp.int32, (experts * cap, 1), 0)
    own_map = sum([(spot_iota == own_ids[k : k + 1] * cap + own_spots[k]).astype(BF) for k in range(top_k)])
    own_sent = dot32(own_map, cotangent).astype(BF)
    own_cot = exchange(own_sent)

    ids = lax.optimization_barrier(ids)
    spots = [spots_of(block) for block in ids]
    slot_iota = lax.broadcasted_iota(jnp.int32, (slots, 1), 0)
    maps = []
    for group in groups:
        by_k = []
        for k in range(top_k):
            target = [
                (ids[j][k : k + 1] // exp_dev) * (exp_dev * seg)
                + (ids[j][k : k + 1] % exp_dev) * seg
                + i * cap
                + spots[j][k]
                for i, j in enumerate(group)
            ]
            by_k.append((slot_iota == jnp.concatenate(target, axis=1)).astype(BF))
        maps.append(by_k)
    merged = [m[0] + m[1] for m in maps]

    def spread(value):
        n = value.shape[1]
        padded = -(-n // 1024) * 1024
        tile = jnp.pad(value, ((0, 0), (0, padded - n))).reshape(-1, 128)
        got = exchange(tile)
        return got.reshape(n_ex, padded)[:, :n]

    others = []
    for group, by_k in zip(groups, maps):
        total = None
        for k in range(top_k):
            value = jnp.concatenate([ids[j][1 - k : 2 - k] for j in group], axis=1).astype(BF)
            term = dot32(value, by_k[k], ((1,), (1,)))
            total = term if total is None else total + term
        others.append(total.reshape(n_ex, exp_dev * seg))
    others = spread(jnp.concatenate(others, axis=1))
    rows = n_ex * seg
    sels = []
    own_expert = ex * exp_dev + lax.broadcasted_iota(jnp.int32, (exp_dev, 1, 1), 0)
    lane_expert = lax.broadcasted_iota(jnp.int32, (1, 1, experts), 2)
    for g in range(len(groups)):
        other = others[:, g * exp_dev * seg : (g + 1) * exp_dev * seg]
        if g == 0:
            other = other.reshape(n_ex, exp_dev, per, cap).transpose(1, 2, 0, 3)
        else:
            other = other.reshape(n_ex, exp_dev, seg).transpose(1, 0, 2)
        other = other.reshape(exp_dev, rows, 1)
        sels.append(
            (lane_expert == own_expert).astype(F32)
            - (lane_expert == other.astype(jnp.int32)).astype(F32)
        )

    def dispatch(blocks, hot):
        sent = dot32(hot, jnp.concatenate(blocks, axis=0)).astype(BF)
        return exchange(sent).reshape(n_ex, exp_dev, seg, width)

    near, far = groups
    line = exp_dev * rows
    at = lax.broadcasted_iota(jnp.int32, (line, 1), 0)
    e_at, blk_at, src_at, pos_at = at // rows, at % rows // (n_ex * cap), at % (n_ex * cap) // cap, at % cap
    came_from = ((blk_at * n_ex + src_at) * exp_dev + e_at) * cap + pos_at
    arrange = (came_from == lax.broadcasted_iota(jnp.int32, (line, line), 1)).astype(BF)

    def gather_near(own):
        every = [own] + [swap(own, "dp", j) for j in near[1:]]
        return dot32(arrange, jnp.concatenate(every, axis=0)).astype(BF).reshape(exp_dev, rows, width)

    cot_near = gather_near(own_cot)
    cots = [swap(cotangent, "dp", j) for j in far]
    slot_cot = [cot_near, dispatch(cots, merged[1])]

    w_dp = jnp.concatenate([w_out] + [swap(w_out, "dp", j) for j in range(1, n_dp)], axis=0)
    from_hi = swap(w_dp, "expert", hi)
    from_lo = swap(w_dp, "expert", lo)
    half_q = rows_q // 2
    diag_a = swap(from_hi[:half_q], "expert", lo)
    diag_b = swap(from_lo[half_q:], "expert", hi)
    w_rel = [jnp.concatenate([w_dp, from_hi, from_lo, diag_a, diag_b], axis=0)]
    bit = lo // 2
    while bit:
        w_rel = w_rel + [swap(piece, "expert", bit) for piece in w_rel]
        bit //= 2

    stream = residual.astype(F32)
    span = w_rel[0].shape[0]
    for i, piece in enumerate(w_rel):
        stream = stream + dot32(ctx_rel[:, i * span : (i + 1) * span], piece)
    average = jnp.mean(stream, axis=1, keepdims=True)
    centred = stream - average
    variance = jnp.mean(centred * centred, axis=1, keepdims=True)
    inv_std = lax.rsqrt(variance + LN_EPS)
    normed = centred * inv_std
    normed_bf = normed.astype(BF)
    xs = [swap(normed_bf, "dp", j) for j in far]
    own_in = exchange(dot32(own_map, normed_bf).astype(BF))
    slot_in = [gather_near(own_in), dispatch(xs, merged[1])]

    normed_rel = dot32(normed_bf, reorder).astype(BF)
    logits = dot32(w_router, normed_bf, ((0,), (1,)))
    late_ids = lax.optimization_barrier(own_ids)
    picks = [(e_iota == late_ids[k : k + 1]).astype(F32) for k in range(top_k)]
    chosen = jnp.concatenate([jnp.sum(h * logits, axis=0, keepdims=True) for h in picks], axis=0)
    gates = jax.nn.sigmoid(chosen - chosen[::-1])

    results = []
    for x, c, sel in zip(slot_in, slot_cot, sels):
        results.append(ffn(x, c, sel, w_router, w_fc1, w_fc2))

    def collect(near_part, far_part):
        pieces = dot32(arrange, near_part.reshape(line, width), ((0,), (0,))).astype(BF)
        size = line // per
        slots_own = pieces[:size].astype(F32)
        for j in near[1:]:
            slots_own = slots_own + swap(pieces[j * size : (j + 1) * size], "dp", j).astype(F32)
        got = exchange(slots_own.astype(BF))
        total = dot32(own_map, got, ((0,), (0,)))
        got = exchange(far_part.reshape(-1, width))
        parts = dot32(merged[1], got, ((0,), (0,))).astype(BF)
        for i, j in enumerate(far):
            total = total + swap(parts[i * tok : (i + 1) * tok], "dp", j).astype(F32)
        return total

    back_sum = collect(results[0][1], results[1][1])
    score = [
        results[0][4].reshape(exp_dev, per, n_ex, cap).transpose(2, 0, 1, 3).reshape(n_ex, exp_dev * seg),
        results[1][4].reshape(exp_dev, n_ex, seg).transpose(1, 0, 2).reshape(n_ex, exp_dev * seg),
    ]
    score = spread(jnp.concatenate(score, axis=1))
    part = exp_dev * seg
    score_parts = []
    for g, by_k in enumerate(maps):
        packed = score[:, g * part : (g + 1) * part].reshape(1, slots)
        both = jnp.concatenate([dot32(packed, by_k[k].astype(F32), precision=HI) for k in range(top_k)], axis=0)
        score_parts += [both[:, i * tok : (i + 1) * tok] for i in range(per)]
    score_sum = score_parts[0]
    for j in range(1, n_dp):
        score_sum = score_sum + swap(score_parts[j], "dp", j)
    mixture = collect(results[0][0], results[1][0])
    d_chosen = score_sum - gates * jnp.sum(score_sum, axis=0, keepdims=True)
    d_logits = sum([picks[k] * d_chosen[k : k + 1] for k in range(top_k)])
    d_normed = back_sum + dot32(d_logits, w_router.astype(F32), ((0,), (1,)), precision=HI)
    cot_float = cotangent.astype(F32)
    d_stream = cot_float + inv_std * (
        d_normed
        - jnp.mean(d_normed, axis=1, keepdims=True)
        - normed * jnp.mean(d_normed * normed, axis=1, keepdims=True)
    )
    d_residual, late_stream = lax.optimization_barrier((d_stream.astype(BF), stream))
    layer_out = (late_stream + mixture).astype(BF)
    d_rel = jnp.concatenate([dot32(d_residual, piece, ((1,), (1,))).astype(BF) for piece in w_rel], axis=1)
    d_context = dot32(d_rel, reorder, ((1,), (1,))).astype(BF)

    rest, thirds = d_logits, []
    for _ in range(3):
        thirds.append(rest.astype(BF))
        rest = rest - thirds[-1].astype(F32)
    thirds = jnp.concatenate(thirds, axis=0)
    thirds = jnp.pad(thirds, ((0, -thirds.shape[0] % 128), (0, 0)))

    def sums_of(cols):
        return [
            dot32(ctx_rel[:, cols], d_residual, ((0,), (0,))),
            dot32(normed_rel[:, cols], thirds, ((0,), (1,))),
        ]

    half = width // 2
    sent = jnp.concatenate([v.astype(BF) for v in sums_of(slice(half, width))], axis=1)
    got = swap(sent, "expert", 1).astype(F32)
    part_out, part_router = sums_of(slice(0, half))
    part_out, part_router = part_out + got[:, :width], part_router + got[:, width:]
    bit = 2
    while bit < lo:
        half = half // 2
        sent = jnp.concatenate([part_out[half:], part_router[half:]], axis=1).astype(BF)
        got = swap(sent, "expert", bit).astype(F32)
        part_out, part_router = part_out[:half] + got[:, :width], part_router[:half] + got[:, width:]
        bit *= 2
    mid = width // 2
    left = [part_out[i * rows_q : (i + 1) * rows_q, :mid] for i in range(4)]
    right = [
        jnp.concatenate([part_out[i * rows_q : (i + 1) * rows_q, mid:], part_router[i * rows_q : (i + 1) * rows_q]], axis=1)
        for i in range(4)
    ]
    got_l = swap(jnp.concatenate([left[2], left[3]], axis=0).astype(BF), "expert", lo).astype(F32)
    got_r = swap(jnp.concatenate([right[1], right[3]], axis=0).astype(BF), "expert", hi).astype(F32)
    fin_l = swap((left[1] + got_l[rows_q:]).astype(BF), "expert", hi).astype(F32)
    fin_r = swap((right[2] + got_r[rows_q:]).astype(BF), "expert", lo).astype(F32)
    kept = jnp.concatenate([left[0] + got_l[:rows_q] + fin_l, right[0] + got_r[:rows_q] + fin_r], axis=1)
    grads = kept[:shard]
    for j in range(1, n_dp):
        grads = grads + swap(kept[j * shard : (j + 1) * shard].astype(BF), "dp", j).astype(F32)
    grads = scale * grads
    grad_out = grads[:, :width]
    grad_router = sum([grads[:, width + i * experts : width + (i + 1) * experts] for i in range(3)])

    grad_fc1 = wgrad(scale, exp_dev, slot_in, [r[3] for r in results])
    grad_fc2 = wgrad(scale, exp_dev, [r[2] for r in results], slot_cot)
    return (layer_out, d_residual, d_context, grad_out, grad_router, grad_fc1, grad_fc2)


def solution(mesh):
    rows = P(("dp", "expert"), None)
    first = P("expert", None, "dp")
    second = P("expert", "dp", None)

    return jax.shard_map(
        on_device,
        mesh=mesh,
        in_specs=(rows, rows, rows, P(), rows, first, second, rows),
        out_specs=(rows, rows, rows, rows, rows, first, second),
        check_vma=False,
    )
```

```python
import functools

import jax
import jax.numpy as jnp
from jax import lax
from jax.experimental import pallas as pl
from jax.experimental.pallas import tpu as pltpu
from jax.sharding import PartitionSpec as P

LN_EPS = 1e-06
BF = jnp.bfloat16
F32 = jnp.float32
HI = lax.Precision.HIGHEST


def dot32(a, b, dims=((1,), (0,)), precision=None):
    return lax.dot_general(
        a, b, (dims, ((), ())), preferred_element_type=F32, precision=precision
    )


def swap(value, axis, bit):
    n = lax.axis_size(axis)
    return lax.ppermute(value, axis, [(i, i ^ bit) for i in range(n)])


def exchange(value):
    return lax.all_to_all(value, "expert", split_axis=0, concat_axis=0, tiled=True)


def chunk_of(size, most):
    for chunk in range(most - most % 128, 0, -128):
        if size % chunk == 0:
            return chunk
    return size


def flat(ref):
    return ref[...].reshape(-1, ref.shape[-1])


def row_block(a, size, step):
    if a.ndim == 3:
        return pl.BlockSpec((None, a.shape[1], size), lambda i, j: (i, 0, j * step))
    return pl.BlockSpec((a.shape[0], None, a.shape[2], size), lambda i, j: (0, i, 0, j * step))


def ffn_kernel(part, x_ref, c_ref, sel_ref, wr_ref, w1_ref, w2_ref, out_ref, back_ref, gh_ref, dp_ref, s_ref, acc_o, acc_b):
    x = flat(x_ref)
    c = flat(c_ref)
    g = jax.nn.sigmoid(jnp.sum(dot32(x, wr_ref[...]) * sel_ref[...], axis=1, keepdims=True))
    count = w1_ref.shape[1] // part
    across = ((1,), (1,))
    spans = [slice(i * part, (i + 1) * part) for i in range(count)]

    def front(span):
        return dot32(x, w1_ref[:, span]), dot32(c, w2_ref[span, :], across)

    score = jnp.zeros_like(g)
    ahead = front(spans[0])
    for i, span in enumerate(spans):
        pre, dh = ahead
        if i + 1 < count:
            ahead = front(spans[i + 1])
        cdf = 0.5 * (1.0 + lax.erf(pre * 0.7071067811865476))
        hid = pre * cdf
        slope = cdf + pre * jnp.exp(-0.5 * pre * pre) * 0.3989422804014327
        dh = dh * g
        dp = (dh * slope).astype(BF)
        score += jnp.sum(dh * hid, axis=1, keepdims=True)
        gh_ref[:, span] = (hid * g).astype(BF)
        dp_ref[:, span] = dp
        out = dot32(hid.astype(BF), w2_ref[span, :])
        back = dot32(dp, w1_ref[:, span], across)
        if i == 0:
            acc_o[...] = out
            acc_b[...] = back
        else:
            acc_o[...] += out
            acc_b[...] += back
    out_ref[...] = (acc_o[...] * g).astype(BF).reshape(out_ref.shape)
    back_ref[...] = acc_b[...].astype(BF).reshape(back_ref.shape)
    s_ref[...] = score


def ffn(x, c, sel, w_router, w1, w2):
    e, width, hidden = w1.shape
    rows = x.size // (e * width)
    experts = w_router.shape[1]
    row_spec = row_block(x, width, 0)

    def own(*shape):
        return pl.BlockSpec((None, *shape), lambda i, j: (i, 0, 0))

    return pl.pallas_call(
        functools.partial(ffn_kernel, chunk_of(hidden, 256)),
        grid=(e, 1),
        in_specs=[
            row_spec,
            row_spec,
            own(rows, experts),
            pl.BlockSpec((width, experts), lambda i, j: (0, 0)),
            own(width, hidden),
            own(hidden, width),
        ],
        out_specs=[row_spec, row_spec, own(rows, hidden), own(rows, hidden), own(rows, 1)],
        out_shape=[
            jax.ShapeDtypeStruct(x.shape, BF),
            jax.ShapeDtypeStruct(x.shape, BF),
            jax.ShapeDtypeStruct((e, rows, hidden), BF),
            jax.ShapeDtypeStruct((e, rows, hidden), BF),
            jax.ShapeDtypeStruct((e, rows, 1), F32),
        ],
        scratch_shapes=[pltpu.VMEM((rows, width), F32), pltpu.VMEM((rows, width), F32)],
        cost_estimate=pl.CostEstimate(
            flops=8 * e * rows * width * hidden,
            bytes_accessed=4 * e * width * hidden + 8 * e * rows * (width + hidden),
            transcendentals=2 * e * rows * hidden,
        ),
        compiler_params=pltpu.CompilerParams(dimension_semantics=("arbitrary", "arbitrary")),
    )(x, c, sel, w_router, w1, w2)


def wgrad_kernel(scale, pairs, *refs):
    left = jnp.concatenate([flat(r) for r in refs[:pairs]], axis=0)
    right = jnp.concatenate([flat(r) for r in refs[pairs:-1]], axis=0)
    refs[-1][0] = dot32(left, right, ((0,), (0,))) * scale


def wgrad(scale, e, lefts, rights):
    m = lefts[0].shape[-1]
    n = rights[0].shape[-1]
    mc = chunk_of(m, 640)
    rows = sum([a.size // (e * m) for a in lefts])
    return pl.pallas_call(
        functools.partial(wgrad_kernel, scale, len(lefts)),
        grid=(e, m // mc),
        in_specs=[row_block(a, mc, 1) for a in lefts] + [row_block(b, n, 0) for b in rights],
        out_specs=pl.BlockSpec((1, mc, n), lambda i, j: (i, j, 0)),
        out_shape=jax.ShapeDtypeStruct((e, m, n), F32),
        cost_estimate=pl.CostEstimate(
            flops=2 * e * rows * m * n,
            bytes_accessed=4 * e * m * n + 2 * e * rows * (m + n),
            transcendentals=0,
        ),
        compiler_params=pltpu.CompilerParams(dimension_semantics=("arbitrary", "arbitrary")),
    )(*lefts, *rights)


def on_device(residual, context, w_out, w_router, expert_ids, w_fc1, w_fc2, cotangent):
    tok, width = residual.shape
    top_k = expert_ids.shape[1]
    n_dp = lax.axis_size("dp")
    n_ex = lax.axis_size("expert")
    z = lax.axis_index("dp")
    ex = lax.axis_index("expert")
    exp_dev = w_fc1.shape[0]
    experts = exp_dev * n_ex
    cap = max(2, (5 * top_k * tok + 4 * experts - 1) // (4 * experts))
    scale = float(tok * n_dp * n_ex) ** (-0.5)
    shard = w_out.shape[0]
    rows_q = n_dp * shard
    hi, lo = n_ex // 2, n_ex // 4
    groups = [list(range(n_dp // 2)), list(range(n_dp // 2, n_dp))]
    per = n_dp // 2
    seg = per * cap
    slots = n_ex * exp_dev * seg

    own_ids = expert_ids.T
    ids = [own_ids] + [swap(own_ids, "dp", j) for j in range(1, n_dp)]

    col = lax.broadcasted_iota(jnp.int32, (1, width), 1)
    place = col // rows_q
    within = col % rows_q
    rel = jnp.zeros_like(place)
    b, m = 1, n_ex // 2
    while m:
        rel = rel + ((place // m) % 2) * b
        b, m = b * 2, m // 2
    source = ((z ^ (within // shard)) * n_ex + (ex ^ rel)) * shard + within % shard
    reorder = (lax.broadcasted_iota(jnp.int32, (width, width), 0) == source).astype(BF)
    ctx_rel = dot32(context, reorder).astype(BF)

    tri = (
        lax.broadcasted_iota(jnp.int32, (tok, tok), 0)
        < lax.broadcasted_iota(jnp.int32, (tok, tok), 1)
    ).astype(BF)
    e_iota = lax.broadcasted_iota(jnp.int32, (experts, tok), 0)

    def spots_of(block):
        hot = [(e_iota == block[k : k + 1]).astype(F32) for k in range(top_k)]
        before = dot32(sum(hot).astype(BF), tri)
        return [jnp.sum(h * before, axis=0, keepdims=True).astype(jnp.int32) for h in hot]

    own_spots = spots_of(own_ids)
    spot_iota = lax.broadcasted_iota(jnp.int32, (experts * cap, 1), 0)
    own_map = sum([(spot_iota == own_ids[k : k + 1] * cap + own_spots[k]).astype(BF) for k in range(top_k)])
    own_sent = dot32(own_map, cotangent).astype(BF)
    own_cot = exchange(own_sent)

    ids = lax.optimization_barrier(ids)
    spots = [spots_of(block) for block in ids]
    slot_iota = lax.broadcasted_iota(jnp.int32, (slots, 1), 0)
    maps = []
    for group in groups:
        by_k = []
        for k in range(top_k):
            target = [
                (ids[j][k : k + 1] // exp_dev) * (exp_dev * seg)
                + (ids[j][k : k + 1] % exp_dev) * seg
                + i * cap
                + spots[j][k]
                for i, j in enumerate(group)
            ]
            by_k.append((slot_iota == jnp.concatenate(target, axis=1)).astype(BF))
        maps.append(by_k)
    merged = [m[0] + m[1] for m in maps]

    def spread(value):
        n = value.shape[1]
        padded = -(-n // 1024) * 1024
        tile = jnp.pad(value, ((0, 0), (0, padded - n))).reshape(-1, 128)
        got = exchange(tile)
        return got.reshape(n_ex, padded)[:, :n]

    others = []
    for group, by_k in zip(groups, maps):
        total = None
        for k in range(top_k):
            value = jnp.concatenate([ids[j][1 - k : 2 - k] for j in group], axis=1).astype(BF)
            term = dot32(value, by_k[k], ((1,), (1,)))
            total = term if total is None else total + term
        others.append(total.reshape(n_ex, exp_dev * seg))
    others = spread(jnp.concatenate(others, axis=1))
    rows = n_ex * seg
    sels = []
    own_expert = ex * exp_dev + lax.broadcasted_iota(jnp.int32, (exp_dev, 1, 1), 0)
    lane_expert = lax.broadcasted_iota(jnp.int32, (1, 1, experts), 2)
    for g in range(len(groups)):
        other = others[:, g * exp_dev * seg : (g + 1) * exp_dev * seg]
        if g == 0:
            other = other.reshape(n_ex, exp_dev, per, cap).transpose(1, 2, 0, 3)
        else:
            other = other.reshape(n_ex, exp_dev, seg).transpose(1, 0, 2)
        other = other.reshape(exp_dev, rows, 1)
        sels.append(
            (lane_expert == own_expert).astype(F32)
            - (lane_expert == other.astype(jnp.int32)).astype(F32)
        )

    def dispatch(blocks, hot):
        sent = dot32(hot, jnp.concatenate(blocks, axis=0)).astype(BF)
        return exchange(sent).reshape(n_ex, exp_dev, seg, width)

    near, far = groups
    line = exp_dev * rows
    at = lax.broadcasted_iota(jnp.int32, (line, 1), 0)
    e_at, blk_at, src_at, pos_at = at // rows, at % rows // (n_ex * cap), at % (n_ex * cap) // cap, at % cap
    came_from = ((blk_at * n_ex + src_at) * exp_dev + e_at) * cap + pos_at
    arrange = (came_from == lax.broadcasted_iota(jnp.int32, (line, line), 1)).astype(BF)

    def gather_near(own):
        every = [own] + [swap(own, "dp", j) for j in near[1:]]
        return dot32(arrange, jnp.concatenate(every, axis=0)).astype(BF).reshape(exp_dev, rows, width)

    cot_near = gather_near(own_cot)
    cots = [swap(cotangent, "dp", j) for j in far]
    slot_cot = [cot_near, dispatch(cots, merged[1])]

    w_dp = jnp.concatenate([w_out] + [swap(w_out, "dp", j) for j in range(1, n_dp)], axis=0)
    from_hi = swap(w_dp, "expert", hi)
    from_lo = swap(w_dp, "expert", lo)
    half_q = rows_q // 2
    diag_a = swap(from_hi[:half_q], "expert", lo)
    diag_b = swap(from_lo[half_q:], "expert", hi)
    w_rel = [jnp.concatenate([w_dp, from_hi, from_lo, diag_a, diag_b], axis=0)]
    bit = lo // 2
    while bit:
        w_rel = w_rel + [swap(piece, "expert", bit) for piece in w_rel]
        bit //= 2

    stream = residual.astype(F32)
    span = w_rel[0].shape[0]
    for i, piece in enumerate(w_rel):
        stream = stream + dot32(ctx_rel[:, i * span : (i + 1) * span], piece)
    average = jnp.mean(stream, axis=1, keepdims=True)
    centred = stream - average
    variance = jnp.mean(centred * centred, axis=1, keepdims=True)
    inv_std = lax.rsqrt(variance + LN_EPS)
    normed = centred * inv_std
    normed_bf = normed.astype(BF)
    xs = [swap(normed_bf, "dp", j) for j in far]
    own_in = exchange(dot32(own_map, normed_bf).astype(BF))
    slot_in = [gather_near(own_in), dispatch(xs, merged[1])]

    normed_rel = dot32(normed_bf, reorder).astype(BF)
    logits = dot32(w_router, normed_bf, ((0,), (1,)))
    late_ids = lax.optimization_barrier(own_ids)
    picks = [(e_iota == late_ids[k : k + 1]).astype(F32) for k in range(top_k)]
    chosen = jnp.concatenate([jnp.sum(h * logits, axis=0, keepdims=True) for h in picks], axis=0)
    gates = jax.nn.sigmoid(chosen - chosen[::-1])

    results = []
    for x, c, sel in zip(slot_in, slot_cot, sels):
        results.append(ffn(x, c, sel, w_router, w_fc1, w_fc2))

    def collect(near_part, far_part):
        pieces = dot32(arrange, near_part.reshape(line, width), ((0,), (0,))).astype(BF)
        size = line // per
        slots_own = pieces[:size].astype(F32)
        for j in near[1:]:
            slots_own = slots_own + swap(pieces[j * size : (j + 1) * size], "dp", j).astype(F32)
        got = exchange(slots_own.astype(BF))
        total = dot32(own_map, got, ((0,), (0,)))
        got = exchange(far_part.reshape(-1, width))
        parts = dot32(merged[1], got, ((0,), (0,))).astype(BF)
        for i, j in enumerate(far):
            total = total + swap(parts[i * tok : (i + 1) * tok], "dp", j).astype(F32)
        return total

    back_sum = collect(results[0][1], results[1][1])
    score = [
        results[0][4].reshape(exp_dev, per, n_ex, cap).transpose(2, 0, 1, 3).reshape(n_ex, exp_dev * seg),
        results[1][4].reshape(exp_dev, n_ex, seg).transpose(1, 0, 2).reshape(n_ex, exp_dev * seg),
    ]
    score = spread(jnp.concatenate(score, axis=1))
    part = exp_dev * seg
    score_parts = []
    for g, by_k in enumerate(maps):
        packed = score[:, g * part : (g + 1) * part].reshape(1, slots)
        both = jnp.concatenate([dot32(packed, by_k[k].astype(F32), precision=HI) for k in range(top_k)], axis=0)
        score_parts += [both[:, i * tok : (i + 1) * tok] for i in range(per)]
    score_sum = score_parts[0]
    for j in range(1, n_dp):
        score_sum = score_sum + swap(score_parts[j], "dp", j)
    mixture = collect(results[0][0], results[1][0])
    d_chosen = score_sum - gates * jnp.sum(score_sum, axis=0, keepdims=True)
    d_logits = sum([picks[k] * d_chosen[k : k + 1] for k in range(top_k)])
    d_normed = back_sum + dot32(d_logits, w_router.astype(F32), ((0,), (1,)), precision=HI)
    cot_float = cotangent.astype(F32)
    d_stream = cot_float + inv_std * (
        d_normed
        - jnp.mean(d_normed, axis=1, keepdims=True)
        - normed * jnp.mean(d_normed * normed, axis=1, keepdims=True)
    )
    d_residual, late_stream = lax.optimization_barrier((d_stream.astype(BF), stream))
    layer_out = (late_stream + mixture).astype(BF)
    d_rel = jnp.concatenate([dot32(d_residual, piece, ((1,), (1,))).astype(BF) for piece in w_rel], axis=1)
    d_context = dot32(d_rel, reorder, ((1,), (1,))).astype(BF)

    rest, thirds = d_logits, []
    for _ in range(3):
        thirds.append(rest.astype(BF))
        rest = rest - thirds[-1].astype(F32)
    thirds = jnp.concatenate(thirds, axis=0)
    thirds = jnp.pad(thirds, ((0, -thirds.shape[0] % 128), (0, 0)))

    def sums_of(cols):
        return [
            dot32(ctx_rel[:, cols], d_residual, ((0,), (0,))),
            dot32(normed_rel[:, cols], thirds, ((0,), (1,))),
        ]

    half = width // 2
    sent = jnp.concatenate([v.astype(BF) for v in sums_of(slice(half, width))], axis=1)
    got = swap(sent, "expert", 1).astype(F32)
    part_out, part_router = sums_of(slice(0, half))
    part_out, part_router = part_out + got[:, :width], part_router + got[:, width:]
    bit = 2
    while bit < lo:
        half = half // 2
        sent = jnp.concatenate([part_out[half:], part_router[half:]], axis=1).astype(BF)
        got = swap(sent, "expert", bit).astype(F32)
        part_out, part_router = part_out[:half] + got[:, :width], part_router[:half] + got[:, width:]
        bit *= 2
    mid = width // 2
    left = [part_out[i * rows_q : (i + 1) * rows_q, :mid] for i in range(4)]
    right = [
        jnp.concatenate([part_out[i * rows_q : (i + 1) * rows_q, mid:], part_router[i * rows_q : (i + 1) * rows_q]], axis=1)
        for i in range(4)
    ]
    got_l = swap(jnp.concatenate([left[2], left[3]], axis=0).astype(BF), "expert", lo).astype(F32)
    got_r = swap(jnp.concatenate([right[1], right[3]], axis=0).astype(BF), "expert", hi).astype(F32)
    fin_l = swap((left[1] + got_l[rows_q:]).astype(BF), "expert", hi).astype(F32)
    fin_r = swap((right[2] + got_r[rows_q:]).astype(BF), "expert", lo).astype(F32)
    kept = jnp.concatenate([left[0] + got_l[:rows_q] + fin_l, right[0] + got_r[:rows_q] + fin_r], axis=1)
    grads = kept[:shard]
    for j in range(1, n_dp):
        grads = grads + swap(kept[j * shard : (j + 1) * shard].astype(BF), "dp", j).astype(F32)
    grads = scale * grads
    grad_out = grads[:, :width]
    grad_router = sum([grads[:, width + i * experts : width + (i + 1) * experts] for i in range(3)])

    grad_fc1 = wgrad(scale, exp_dev, slot_in, [r[3] for r in results])
    grad_fc2 = wgrad(scale, exp_dev, [r[2] for r in results], slot_cot)
    return (layer_out, d_residual, d_context, grad_out, grad_router, grad_fc1, grad_fc2)


def solution(mesh):
    rows = P(("dp", "expert"), None)
    first = P("expert", None, "dp")
    second = P("expert", "dp", None)

    return jax.shard_map(
        on_device,
        mesh=mesh,
        in_specs=(rows, rows, rows, P(), rows, first, second, rows),
        out_specs=(rows, rows, rows, rows, rows, first, second),
        check_vma=False,
    )
```

```python
import functools

import jax
import jax.numpy as jnp
from jax import lax
from jax.experimental import pallas as pl
from jax.experimental.pallas import tpu as pltpu
from jax.sharding import PartitionSpec as P

LN_EPS = 1e-06
BF = jnp.bfloat16
F32 = jnp.float32
HI = lax.Precision.HIGHEST


def dot32(a, b, dims=((1,), (0,)), precision=None):
    return lax.dot_general(
        a, b, (dims, ((), ())), preferred_element_type=F32, precision=precision
    )


def swap(value, axis, bit):
    n = lax.axis_size(axis)
    return lax.ppermute(value, axis, [(i, i ^ bit) for i in range(n)])


def exchange(value):
    return lax.all_to_all(value, "expert", split_axis=0, concat_axis=0, tiled=True)


def chunk_of(size, most):
    for chunk in range(most - most % 128, 0, -128):
        if size % chunk == 0:
            return chunk
    return size


def flat(ref):
    return ref[...].reshape(-1, ref.shape[-1])


def row_block(a, size, step):
    if a.ndim == 3:
        return pl.BlockSpec((None, a.shape[1], size), lambda i, j: (i, 0, j * step))
    return pl.BlockSpec((a.shape[0], None, a.shape[2], size), lambda i, j: (0, i, 0, j * step))


def ffn_kernel(part, x_ref, c_ref, sel_ref, wr_ref, w1_ref, w2_ref, out_ref, back_ref, gh_ref, dp_ref, s_ref, acc_o, acc_b):
    x = flat(x_ref)
    c = flat(c_ref)
    g = jax.nn.sigmoid(jnp.sum(dot32(x, wr_ref[...]) * sel_ref[...], axis=1, keepdims=True))
    count = w1_ref.shape[1] // part
    across = ((1,), (1,))
    acc_o[...] = jnp.zeros_like(acc_o)
    acc_b[...] = jnp.zeros_like(acc_b)

    def body(i, score):
        span = pl.ds(pl.multiple_of(i * part, part), part)
        pre = dot32(x, w1_ref[:, span])
        dh = dot32(c, w2_ref[span, :], across) * g
        cdf = 0.5 * (1.0 + lax.erf(pre * 0.7071067811865476))
        hid = pre * cdf
        slope = cdf + pre * jnp.exp(-0.5 * pre * pre) * 0.3989422804014327
        dp = (dh * slope).astype(BF)
        gh_ref[:, span] = (hid * g).astype(BF)
        dp_ref[:, span] = dp
        acc_o[...] += dot32(hid.astype(BF), w2_ref[span, :])
        acc_b[...] += dot32(dp, w1_ref[:, span], across)
        return score + jnp.sum(dh * hid, axis=1, keepdims=True)

    score = lax.fori_loop(0, count, body, jnp.zeros_like(g))
    out_ref[...] = (acc_o[...] * g).astype(BF).reshape(out_ref.shape)
    back_ref[...] = acc_b[...].astype(BF).reshape(back_ref.shape)
    s_ref[...] = score


def ffn(x, c, sel, w_router, w1, w2):
    e, width, hidden = w1.shape
    rows = x.size // (e * width)
    experts = w_router.shape[1]
    row_spec = row_block(x, width, 0)

    def own(*shape):
        return pl.BlockSpec((None, *shape), lambda i, j: (i, 0, 0))

    return pl.pallas_call(
        functools.partial(ffn_kernel, chunk_of(hidden, 256)),
        grid=(e, 1),
        in_specs=[
            row_spec,
            row_spec,
            own(rows, experts),
            pl.BlockSpec((width, experts), lambda i, j: (0, 0)),
            own(width, hidden),
            own(hidden, width),
        ],
        out_specs=[row_spec, row_spec, own(rows, hidden), own(rows, hidden), own(rows, 1)],
        out_shape=[
            jax.ShapeDtypeStruct(x.shape, BF),
            jax.ShapeDtypeStruct(x.shape, BF),
            jax.ShapeDtypeStruct((e, rows, hidden), BF),
            jax.ShapeDtypeStruct((e, rows, hidden), BF),
            jax.ShapeDtypeStruct((e, rows, 1), F32),
        ],
        scratch_shapes=[pltpu.VMEM((rows, width), F32), pltpu.VMEM((rows, width), F32)],
        cost_estimate=pl.CostEstimate(
            flops=8 * e * rows * width * hidden,
            bytes_accessed=4 * e * width * hidden + 8 * e * rows * (width + hidden),
            transcendentals=2 * e * rows * hidden,
        ),
        compiler_params=pltpu.CompilerParams(dimension_semantics=("arbitrary", "arbitrary")),
    )(x, c, sel, w_router, w1, w2)


def wgrad_kernel(scale, pairs, *refs):
    left = jnp.concatenate([flat(r) for r in refs[:pairs]], axis=0)
    right = jnp.concatenate([flat(r) for r in refs[pairs:-1]], axis=0)
    refs[-1][0] = dot32(left, right, ((0,), (0,))) * scale


def wgrad(scale, e, lefts, rights):
    m = lefts[0].shape[-1]
    n = rights[0].shape[-1]
    mc = chunk_of(m, 640)
    rows = sum([a.size // (e * m) for a in lefts])
    return pl.pallas_call(
        functools.partial(wgrad_kernel, scale, len(lefts)),
        grid=(e, m // mc),
        in_specs=[row_block(a, mc, 1) for a in lefts] + [row_block(b, n, 0) for b in rights],
        out_specs=pl.BlockSpec((1, mc, n), lambda i, j: (i, j, 0)),
        out_shape=jax.ShapeDtypeStruct((e, m, n), F32),
        cost_estimate=pl.CostEstimate(
            flops=2 * e * rows * m * n,
            bytes_accessed=4 * e * m * n + 2 * e * rows * (m + n),
            transcendentals=0,
        ),
        compiler_params=pltpu.CompilerParams(dimension_semantics=("arbitrary", "arbitrary")),
    )(*lefts, *rights)


def on_device(residual, context, w_out, w_router, expert_ids, w_fc1, w_fc2, cotangent):
    tok, width = residual.shape
    top_k = expert_ids.shape[1]
    n_dp = lax.axis_size("dp")
    n_ex = lax.axis_size("expert")
    z = lax.axis_index("dp")
    ex = lax.axis_index("expert")
    exp_dev = w_fc1.shape[0]
    experts = exp_dev * n_ex
    cap = max(2, (5 * top_k * tok + 4 * experts - 1) // (4 * experts))
    scale = float(tok * n_dp * n_ex) ** (-0.5)
    shard = w_out.shape[0]
    rows_q = n_dp * shard
    hi, lo = n_ex // 2, n_ex // 4
    groups = [list(range(n_dp // 2)), list(range(n_dp // 2, n_dp))]
    per = n_dp // 2
    seg = per * cap
    slots = n_ex * exp_dev * seg

    own_ids = expert_ids.T
    ids = [own_ids] + [swap(own_ids, "dp", j) for j in range(1, n_dp)]

    col = lax.broadcasted_iota(jnp.int32, (1, width), 1)
    place = col // rows_q
    within = col % rows_q
    rel = jnp.zeros_like(place)
    b, m = 1, n_ex // 2
    while m:
        rel = rel + ((place // m) % 2) * b
        b, m = b * 2, m // 2
    source = ((z ^ (within // shard)) * n_ex + (ex ^ rel)) * shard + within % shard
    reorder = (lax.broadcasted_iota(jnp.int32, (width, width), 0) == source).astype(BF)
    ctx_rel = dot32(context, reorder).astype(BF)

    tri = (
        lax.broadcasted_iota(jnp.int32, (tok, tok), 0)
        < lax.broadcasted_iota(jnp.int32, (tok, tok), 1)
    ).astype(BF)
    e_iota = lax.broadcasted_iota(jnp.int32, (experts, tok), 0)

    def spots_of(block):
        hot = [(e_iota == block[k : k + 1]).astype(F32) for k in range(top_k)]
        before = dot32(sum(hot).astype(BF), tri)
        return [jnp.sum(h * before, axis=0, keepdims=True).astype(jnp.int32) for h in hot]

    own_spots = spots_of(own_ids)
    spot_iota = lax.broadcasted_iota(jnp.int32, (experts * cap, 1), 0)
    own_map = sum([(spot_iota == own_ids[k : k + 1] * cap + own_spots[k]).astype(BF) for k in range(top_k)])
    own_sent = dot32(own_map, cotangent).astype(BF)
    own_cot = exchange(own_sent)

    ids = lax.optimization_barrier(ids)
    spots = [spots_of(block) for block in ids]
    slot_iota = lax.broadcasted_iota(jnp.int32, (slots, 1), 0)
    maps = []
    for group in groups:
        by_k = []
        for k in range(top_k):
            target = [
                (ids[j][k : k + 1] // exp_dev) * (exp_dev * seg)
                + (ids[j][k : k + 1] % exp_dev) * seg
                + i * cap
                + spots[j][k]
                for i, j in enumerate(group)
            ]
            by_k.append((slot_iota == jnp.concatenate(target, axis=1)).astype(BF))
        maps.append(by_k)
    merged = [m[0] + m[1] for m in maps]

    def spread(value):
        n = value.shape[1]
        padded = -(-n // 1024) * 1024
        tile = jnp.pad(value, ((0, 0), (0, padded - n))).reshape(-1, 128)
        got = exchange(tile)
        return got.reshape(n_ex, padded)[:, :n]

    others = []
    for group, by_k in zip(groups, maps):
        total = None
        for k in range(top_k):
            value = jnp.concatenate([ids[j][1 - k : 2 - k] for j in group], axis=1).astype(BF)
            term = dot32(value, by_k[k], ((1,), (1,)))
            total = term if total is None else total + term
        others.append(total.reshape(n_ex, exp_dev * seg))
    others = spread(jnp.concatenate(others, axis=1))
    rows = n_ex * seg
    sels = []
    own_expert = ex * exp_dev + lax.broadcasted_iota(jnp.int32, (exp_dev, 1, 1), 0)
    lane_expert = lax.broadcasted_iota(jnp.int32, (1, 1, experts), 2)
    for g in range(len(groups)):
        other = others[:, g * exp_dev * seg : (g + 1) * exp_dev * seg]
        if g == 0:
            other = other.reshape(n_ex, exp_dev, per, cap).transpose(1, 2, 0, 3)
        else:
            other = other.reshape(n_ex, exp_dev, seg).transpose(1, 0, 2)
        other = other.reshape(exp_dev, rows, 1)
        sels.append(
            (lane_expert == own_expert).astype(F32)
            - (lane_expert == other.astype(jnp.int32)).astype(F32)
        )

    def dispatch(blocks, hot):
        sent = dot32(hot, jnp.concatenate(blocks, axis=0)).astype(BF)
        return exchange(sent).reshape(n_ex, exp_dev, seg, width)

    near, far = groups
    line = exp_dev * rows
    at = lax.broadcasted_iota(jnp.int32, (line, 1), 0)
    e_at, blk_at, src_at, pos_at = at // rows, at % rows // (n_ex * cap), at % (n_ex * cap) // cap, at % cap
    came_from = ((blk_at * n_ex + src_at) * exp_dev + e_at) * cap + pos_at
    arrange = (came_from == lax.broadcasted_iota(jnp.int32, (line, line), 1)).astype(BF)

    def gather_near(own):
        every = [own] + [swap(own, "dp", j) for j in near[1:]]
        return dot32(arrange, jnp.concatenate(every, axis=0)).astype(BF).reshape(exp_dev, rows, width)

    cot_near = gather_near(own_cot)
    cots = [swap(cotangent, "dp", j) for j in far]
    slot_cot = [cot_near, dispatch(cots, merged[1])]

    w_dp = jnp.concatenate([w_out] + [swap(w_out, "dp", j) for j in range(1, n_dp)], axis=0)
    from_hi = swap(w_dp, "expert", hi)
    from_lo = swap(w_dp, "expert", lo)
    half_q = rows_q // 2
    diag_a = swap(from_hi[:half_q], "expert", lo)
    diag_b = swap(from_lo[half_q:], "expert", hi)
    w_rel = [jnp.concatenate([w_dp, from_hi, from_lo, diag_a, diag_b], axis=0)]
    bit = lo // 2
    while bit:
        w_rel = w_rel + [swap(piece, "expert", bit) for piece in w_rel]
        bit //= 2

    stream = residual.astype(F32)
    span = w_rel[0].shape[0]
    for i, piece in enumerate(w_rel):
        stream = stream + dot32(ctx_rel[:, i * span : (i + 1) * span], piece)
    average = jnp.mean(stream, axis=1, keepdims=True)
    centred = stream - average
    variance = jnp.mean(centred * centred, axis=1, keepdims=True)
    inv_std = lax.rsqrt(variance + LN_EPS)
    normed = centred * inv_std
    normed_bf = normed.astype(BF)
    xs = [swap(normed_bf, "dp", j) for j in far]
    own_in = exchange(dot32(own_map, normed_bf).astype(BF))
    slot_in = [gather_near(own_in), dispatch(xs, merged[1])]

    normed_rel = dot32(normed_bf, reorder).astype(BF)
    logits = dot32(w_router, normed_bf, ((0,), (1,)))
    late_ids = lax.optimization_barrier(own_ids)
    picks = [(e_iota == late_ids[k : k + 1]).astype(F32) for k in range(top_k)]
    chosen = jnp.concatenate([jnp.sum(h * logits, axis=0, keepdims=True) for h in picks], axis=0)
    gates = jax.nn.sigmoid(chosen - chosen[::-1])

    results = []
    for x, c, sel in zip(slot_in, slot_cot, sels):
        results.append(ffn(x, c, sel, w_router, w_fc1, w_fc2))

    def collect(near_part, far_part):
        pieces = dot32(arrange, near_part.reshape(line, width), ((0,), (0,))).astype(BF)
        size = line // per
        slots_own = pieces[:size].astype(F32)
        for j in near[1:]:
            slots_own = slots_own + swap(pieces[j * size : (j + 1) * size], "dp", j).astype(F32)
        got = exchange(slots_own.astype(BF))
        total = dot32(own_map, got, ((0,), (0,)))
        got = exchange(far_part.reshape(-1, width))
        parts = dot32(merged[1], got, ((0,), (0,))).astype(BF)
        for i, j in enumerate(far):
            total = total + swap(parts[i * tok : (i + 1) * tok], "dp", j).astype(F32)
        return total

    back_sum = collect(results[0][1], results[1][1])
    score = [
        results[0][4].reshape(exp_dev, per, n_ex, cap).transpose(2, 0, 1, 3).reshape(n_ex, exp_dev * seg),
        results[1][4].reshape(exp_dev, n_ex, seg).transpose(1, 0, 2).reshape(n_ex, exp_dev * seg),
    ]
    score = spread(jnp.concatenate(score, axis=1))
    part = exp_dev * seg
    score_parts = []
    for g, by_k in enumerate(maps):
        packed = score[:, g * part : (g + 1) * part].reshape(1, slots)
        both = jnp.concatenate([dot32(packed, by_k[k].astype(F32), precision=HI) for k in range(top_k)], axis=0)
        score_parts += [both[:, i * tok : (i + 1) * tok] for i in range(per)]
    score_sum = score_parts[0]
    for j in range(1, n_dp):
        score_sum = score_sum + swap(score_parts[j], "dp", j)
    mixture = collect(results[0][0], results[1][0])
    d_chosen = score_sum - gates * jnp.sum(score_sum, axis=0, keepdims=True)
    d_logits = sum([picks[k] * d_chosen[k : k + 1] for k in range(top_k)])
    d_normed = back_sum + dot32(d_logits, w_router.astype(F32), ((0,), (1,)), precision=HI)
    cot_float = cotangent.astype(F32)
    d_stream = cot_float + inv_std * (
        d_normed
        - jnp.mean(d_normed, axis=1, keepdims=True)
        - normed * jnp.mean(d_normed * normed, axis=1, keepdims=True)
    )
    d_residual, late_stream = lax.optimization_barrier((d_stream.astype(BF), stream))
    layer_out = (late_stream + mixture).astype(BF)
    d_rel = jnp.concatenate([dot32(d_residual, piece, ((1,), (1,))).astype(BF) for piece in w_rel], axis=1)
    d_context = dot32(d_rel, reorder, ((1,), (1,))).astype(BF)

    rest, thirds = d_logits, []
    for _ in range(3):
        thirds.append(rest.astype(BF))
        rest = rest - thirds[-1].astype(F32)
    thirds = jnp.concatenate(thirds, axis=0)
    thirds = jnp.pad(thirds, ((0, -thirds.shape[0] % 128), (0, 0)))

    def sums_of(cols):
        return [
            dot32(ctx_rel[:, cols], d_residual, ((0,), (0,))),
            dot32(normed_rel[:, cols], thirds, ((0,), (1,))),
        ]

    half = width // 2
    sent = jnp.concatenate([v.astype(BF) for v in sums_of(slice(half, width))], axis=1)
    got = swap(sent, "expert", 1).astype(F32)
    part_out, part_router = sums_of(slice(0, half))
    part_out, part_router = part_out + got[:, :width], part_router + got[:, width:]
    bit = 2
    while bit < lo:
        half = half // 2
        sent = jnp.concatenate([part_out[half:], part_router[half:]], axis=1).astype(BF)
        got = swap(sent, "expert", bit).astype(F32)
        part_out, part_router = part_out[:half] + got[:, :width], part_router[:half] + got[:, width:]
        bit *= 2
    mid = width // 2
    left = [part_out[i * rows_q : (i + 1) * rows_q, :mid] for i in range(4)]
    right = [
        jnp.concatenate([part_out[i * rows_q : (i + 1) * rows_q, mid:], part_router[i * rows_q : (i + 1) * rows_q]], axis=1)
        for i in range(4)
    ]
    got_l = swap(jnp.concatenate([left[2], left[3]], axis=0).astype(BF), "expert", lo).astype(F32)
    got_r = swap(jnp.concatenate([right[1], right[3]], axis=0).astype(BF), "expert", hi).astype(F32)
    fin_l = swap((left[1] + got_l[rows_q:]).astype(BF), "expert", hi).astype(F32)
    fin_r = swap((right[2] + got_r[rows_q:]).astype(BF), "expert", lo).astype(F32)
    kept = jnp.concatenate([left[0] + got_l[:rows_q] + fin_l, right[0] + got_r[:rows_q] + fin_r], axis=1)
    grads = kept[:shard]
    for j in range(1, n_dp):
        grads = grads + swap(kept[j * shard : (j + 1) * shard].astype(BF), "dp", j).astype(F32)
    grads = scale * grads
    grad_out = grads[:, :width]
    grad_router = sum([grads[:, width + i * experts : width + (i + 1) * experts] for i in range(3)])

    grad_fc1 = wgrad(scale, exp_dev, slot_in, [r[3] for r in results])
    grad_fc2 = wgrad(scale, exp_dev, [r[2] for r in results], slot_cot)
    return (layer_out, d_residual, d_context, grad_out, grad_router, grad_fc1, grad_fc2)


def solution(mesh):
    rows = P(("dp", "expert"), None)
    first = P("expert", None, "dp")
    second = P("expert", "dp", None)

    return jax.shard_map(
        on_device,
        mesh=mesh,
        in_specs=(rows, rows, rows, P(), rows, first, second, rows),
        out_specs=(rows, rows, rows, rows, rows, first, second),
        check_vma=False,
    )
```

```python
import functools

import jax
import jax.numpy as jnp
from jax import lax
from jax.experimental import pallas as pl
from jax.experimental.pallas import tpu as pltpu
from jax.sharding import PartitionSpec as P

LN_EPS = 1e-06
BF = jnp.bfloat16
F32 = jnp.float32
HI = lax.Precision.HIGHEST


def dot32(a, b, dims=((1,), (0,)), precision=None):
    return lax.dot_general(
        a, b, (dims, ((), ())), preferred_element_type=F32, precision=precision
    )


def swap(value, axis, bit):
    n = lax.axis_size(axis)
    return lax.ppermute(value, axis, [(i, i ^ bit) for i in range(n)])


def exchange(value):
    return lax.all_to_all(value, "expert", split_axis=0, concat_axis=0, tiled=True)


def chunk_of(size, most):
    for chunk in range(most - most % 128, 0, -128):
        if size % chunk == 0:
            return chunk
    return size


def flat(ref):
    return ref[...].reshape(-1, ref.shape[-1])


def row_block(a, size, step):
    if a.ndim == 3:
        return pl.BlockSpec((None, a.shape[1], size), lambda i, j: (i, 0, j * step))
    return pl.BlockSpec((a.shape[0], None, a.shape[2], size), lambda i, j: (0, i, 0, j * step))


def ffn_kernel(part, x_ref, c_ref, sel_ref, wr_ref, w1_ref, w2_ref, out_ref, back_ref, gh_ref, dp_ref, s_ref, acc_o, acc_b):
    x = flat(x_ref)
    c = flat(c_ref)
    g = jax.nn.sigmoid(jnp.sum(dot32(x, wr_ref[...]) * sel_ref[...], axis=1, keepdims=True))
    count = w1_ref.shape[1] // part
    across = ((1,), (1,))
    acc_o[...] = jnp.zeros_like(acc_o)
    acc_b[...] = jnp.zeros_like(acc_b)

    def body(i, score):
        span = pl.ds(pl.multiple_of(i * part, part), part)
        pre = dot32(x, w1_ref[:, span])
        dh = dot32(c, w2_ref[span, :], across) * g
        cdf = 0.5 * (1.0 + lax.erf(pre * 0.7071067811865476))
        hid = pre * cdf
        slope = cdf + pre * jnp.exp(-0.5 * pre * pre) * 0.3989422804014327
        dp = (dh * slope).astype(BF)
        gh_ref[:, span] = (hid * g).astype(BF)
        dp_ref[:, span] = dp
        acc_o[...] += dot32(hid.astype(BF), w2_ref[span, :])
        acc_b[...] += dot32(dp, w1_ref[:, span], across)
        return score + jnp.sum(dh * hid, axis=1, keepdims=True)

    score = lax.fori_loop(0, count, body, jnp.zeros_like(g))
    out_ref[...] = (acc_o[...] * g).astype(BF).reshape(out_ref.shape)
    back_ref[...] = acc_b[...].astype(BF).reshape(back_ref.shape)
    s_ref[...] = score


def ffn(x, c, sel, w_router, w1, w2):
    e, width, hidden = w1.shape
    rows = x.size // (e * width)
    experts = w_router.shape[1]
    row_spec = row_block(x, width, 0)

    def own(*shape):
        return pl.BlockSpec((None, *shape), lambda i, j: (i, 0, 0))

    return pl.pallas_call(
        functools.partial(ffn_kernel, chunk_of(hidden, 256)),
        grid=(e, 1),
        in_specs=[
            row_spec,
            row_spec,
            own(rows, experts),
            pl.BlockSpec((width, experts), lambda i, j: (0, 0)),
            own(width, hidden),
            own(hidden, width),
        ],
        out_specs=[row_spec, row_spec, own(rows, hidden), own(rows, hidden), own(rows, 1)],
        out_shape=[
            jax.ShapeDtypeStruct(x.shape, BF),
            jax.ShapeDtypeStruct(x.shape, BF),
            jax.ShapeDtypeStruct((e, rows, hidden), BF),
            jax.ShapeDtypeStruct((e, rows, hidden), BF),
            jax.ShapeDtypeStruct((e, rows, 1), F32),
        ],
        scratch_shapes=[pltpu.VMEM((rows, width), F32), pltpu.VMEM((rows, width), F32)],
        cost_estimate=pl.CostEstimate(
            flops=8 * e * rows * width * hidden,
            bytes_accessed=4 * e * width * hidden + 8 * e * rows * (width + hidden),
            transcendentals=2 * e * rows * hidden,
        ),
        compiler_params=pltpu.CompilerParams(dimension_semantics=("arbitrary", "arbitrary")),
    )(x, c, sel, w_router, w1, w2)


def wgrad_kernel(scale, pairs, *refs):
    left = jnp.concatenate([flat(r) for r in refs[:pairs]], axis=0)
    right = jnp.concatenate([flat(r) for r in refs[pairs:-1]], axis=0)
    refs[-1][0] = dot32(left, right, ((0,), (0,))) * scale


def wgrad(scale, e, lefts, rights):
    m = lefts[0].shape[-1]
    n = rights[0].shape[-1]
    mc = chunk_of(m, 640)
    rows = sum([a.size // (e * m) for a in lefts])
    return pl.pallas_call(
        functools.partial(wgrad_kernel, scale, len(lefts)),
        grid=(e, m // mc),
        in_specs=[row_block(a, mc, 1) for a in lefts] + [row_block(b, n, 0) for b in rights],
        out_specs=pl.BlockSpec((1, mc, n), lambda i, j: (i, j, 0)),
        out_shape=jax.ShapeDtypeStruct((e, m, n), F32),
        cost_estimate=pl.CostEstimate(
            flops=2 * e * rows * m * n,
            bytes_accessed=4 * e * m * n + 2 * e * rows * (m + n),
            transcendentals=0,
        ),
        compiler_params=pltpu.CompilerParams(dimension_semantics=("arbitrary", "arbitrary")),
    )(*lefts, *rights)


def on_device(residual, context, w_out, w_router, expert_ids, w_fc1, w_fc2, cotangent):
    tok, width = residual.shape
    top_k = expert_ids.shape[1]
    n_dp = lax.axis_size("dp")
    n_ex = lax.axis_size("expert")
    z = lax.axis_index("dp")
    ex = lax.axis_index("expert")
    exp_dev = w_fc1.shape[0]
    experts = exp_dev * n_ex
    cap = max(2, (5 * top_k * tok + 4 * experts - 1) // (4 * experts))
    scale = float(tok * n_dp * n_ex) ** (-0.5)
    shard = w_out.shape[0]
    rows_q = n_dp * shard
    hi, lo = n_ex // 2, n_ex // 4
    groups = [list(range(n_dp // 2)), list(range(n_dp // 2, n_dp))]
    per = n_dp // 2
    seg = per * cap
    slots = n_ex * exp_dev * seg

    own_ids = expert_ids.T
    ids = [own_ids] + [swap(own_ids, "dp", j) for j in range(1, n_dp)]

    col = lax.broadcasted_iota(jnp.int32, (1, width), 1)
    place = col // rows_q
    within = col % rows_q
    rel = jnp.zeros_like(place)
    b, m = 1, n_ex // 2
    while m:
        rel = rel + ((place // m) % 2) * b
        b, m = b * 2, m // 2
    source = ((z ^ (within // shard)) * n_ex + (ex ^ rel)) * shard + within % shard
    reorder = (lax.broadcasted_iota(jnp.int32, (width, width), 0) == source).astype(BF)
    ctx_rel = dot32(context, reorder).astype(BF)

    tri = (
        lax.broadcasted_iota(jnp.int32, (tok, tok), 0)
        < lax.broadcasted_iota(jnp.int32, (tok, tok), 1)
    ).astype(BF)
    e_iota = lax.broadcasted_iota(jnp.int32, (experts, tok), 0)

    def spots_of(block):
        hot = [(e_iota == block[k : k + 1]).astype(F32) for k in range(top_k)]
        before = dot32(sum(hot).astype(BF), tri)
        return [jnp.sum(h * before, axis=0, keepdims=True).astype(jnp.int32) for h in hot]

    own_spots = spots_of(own_ids)
    spot_iota = lax.broadcasted_iota(jnp.int32, (experts * cap, 1), 0)
    own_map = sum([(spot_iota == own_ids[k : k + 1] * cap + own_spots[k]).astype(BF) for k in range(top_k)])
    own_sent = dot32(own_map, cotangent).astype(BF)
    own_cot = exchange(own_sent)

    ids = lax.optimization_barrier(ids)
    spots = [spots_of(block) for block in ids]
    slot_iota = lax.broadcasted_iota(jnp.int32, (slots, 1), 0)
    maps = []
    for group in groups:
        by_k = []
        for k in range(top_k):
            target = [
                (ids[j][k : k + 1] // exp_dev) * (exp_dev * seg)
                + (ids[j][k : k + 1] % exp_dev) * seg
                + i * cap
                + spots[j][k]
                for i, j in enumerate(group)
            ]
            by_k.append((slot_iota == jnp.concatenate(target, axis=1)).astype(BF))
        maps.append(by_k)
    merged = [m[0] + m[1] for m in maps]

    def spread(value):
        n = value.shape[1]
        padded = -(-n // 1024) * 1024
        tile = jnp.pad(value, ((0, 0), (0, padded - n))).reshape(-1, 128)
        got = exchange(tile)
        return got.reshape(n_ex, padded)[:, :n]

    others = []
    for group, by_k in zip(groups, maps):
        total = None
        for k in range(top_k):
            value = jnp.concatenate([ids[j][1 - k : 2 - k] for j in group], axis=1).astype(BF)
            term = dot32(value, by_k[k], ((1,), (1,)))
            total = term if total is None else total + term
        others.append(total.reshape(n_ex, exp_dev * seg))
    others = spread(jnp.concatenate(others, axis=1))
    rows = n_ex * seg
    sels = []
    own_expert = ex * exp_dev + lax.broadcasted_iota(jnp.int32, (exp_dev, 1, 1), 0)
    lane_expert = lax.broadcasted_iota(jnp.int32, (1, 1, experts), 2)
    for g in range(len(groups)):
        other = others[:, g * exp_dev * seg : (g + 1) * exp_dev * seg]
        if g == 0:
            other = other.reshape(n_ex, exp_dev, per, cap).transpose(1, 2, 0, 3)
        else:
            other = other.reshape(n_ex, exp_dev, seg).transpose(1, 0, 2)
        other = other.reshape(exp_dev, rows, 1)
        sels.append(
            (lane_expert == own_expert).astype(F32)
            - (lane_expert == other.astype(jnp.int32)).astype(F32)
        )

    def dispatch(blocks, hot):
        sent = dot32(hot, jnp.concatenate(blocks, axis=0)).astype(BF)
        return exchange(sent).reshape(n_ex, exp_dev, seg, width)

    near, far = groups
    line = exp_dev * rows
    at = lax.broadcasted_iota(jnp.int32, (line, 1), 0)
    e_at, blk_at, src_at, pos_at = at // rows, at % rows // (n_ex * cap), at % (n_ex * cap) // cap, at % cap
    came_from = ((blk_at * n_ex + src_at) * exp_dev + e_at) * cap + pos_at
    arrange = (came_from == lax.broadcasted_iota(jnp.int32, (line, line), 1)).astype(BF)

    def gather_near(own):
        every = [own] + [swap(own, "dp", j) for j in near[1:]]
        return dot32(arrange, jnp.concatenate(every, axis=0)).astype(BF).reshape(exp_dev, rows, width)

    cot_near = gather_near(own_cot)
    cots = [swap(cotangent, "dp", j) for j in far]
    slot_cot = [cot_near, dispatch(cots, merged[1])]

    w_dp = jnp.concatenate([w_out] + [swap(w_out, "dp", j) for j in range(1, n_dp)], axis=0)
    from_hi = swap(w_dp, "expert", hi)
    from_lo = swap(w_dp, "expert", lo)
    half_q = rows_q // 2
    diag_a = swap(from_hi[:half_q], "expert", lo)
    diag_b = swap(from_lo[half_q:], "expert", hi)
    w_rel = [jnp.concatenate([w_dp, from_hi, from_lo, diag_a, diag_b], axis=0)]
    bit = lo // 2
    while bit:
        w_rel = w_rel + [swap(piece, "expert", bit) for piece in w_rel]
        bit //= 2

    stream = residual.astype(F32)
    span = w_rel[0].shape[0]
    for i, piece in enumerate(w_rel):
        stream = stream + dot32(ctx_rel[:, i * span : (i + 1) * span], piece)
    average = jnp.mean(stream, axis=1, keepdims=True)
    centred = stream - average
    variance = jnp.mean(centred * centred, axis=1, keepdims=True)
    inv_std = lax.rsqrt(variance + LN_EPS)
    normed = centred * inv_std
    normed_bf = normed.astype(BF)
    xs = [swap(normed_bf, "dp", j) for j in far]
    own_in = exchange(dot32(own_map, normed_bf).astype(BF))
    slot_in = [gather_near(own_in), dispatch(xs, merged[1])]

    normed_rel = dot32(normed_bf, reorder).astype(BF)
    logits = dot32(w_router, normed_bf, ((0,), (1,)))
    late_ids = lax.optimization_barrier(own_ids)
    picks = [(e_iota == late_ids[k : k + 1]).astype(F32) for k in range(top_k)]
    chosen = jnp.concatenate([jnp.sum(h * logits, axis=0, keepdims=True) for h in picks], axis=0)
    gates = jax.nn.sigmoid(chosen - chosen[::-1])

    results = []
    for x, c, sel in zip(slot_in, slot_cot, sels):
        results.append(ffn(x, c, sel, w_router, w_fc1, w_fc2))

    def collect(near_part, far_part):
        pieces = dot32(arrange, near_part.reshape(line, width), ((0,), (0,))).astype(BF)
        size = line // per
        slots_own = pieces[:size].astype(F32)
        for j in near[1:]:
            slots_own = slots_own + swap(pieces[j * size : (j + 1) * size], "dp", j).astype(F32)
        got = exchange(slots_own.astype(BF))
        total = dot32(own_map, got, ((0,), (0,)))
        got = exchange(far_part.reshape(-1, width))
        parts = dot32(merged[1], got, ((0,), (0,))).astype(BF)
        for i, j in enumerate(far):
            total = total + swap(parts[i * tok : (i + 1) * tok], "dp", j).astype(F32)
        return total

    back_sum = collect(results[0][1], results[1][1])
    score = [
        results[0][4].reshape(exp_dev, per, n_ex, cap).transpose(2, 0, 1, 3).reshape(n_ex, exp_dev * seg),
        results[1][4].reshape(exp_dev, n_ex, seg).transpose(1, 0, 2).reshape(n_ex, exp_dev * seg),
    ]
    score = spread(jnp.concatenate(score, axis=1))
    part = exp_dev * seg
    score_parts = []
    for g, by_k in enumerate(maps):
        packed = score[:, g * part : (g + 1) * part].reshape(1, slots)
        both = jnp.concatenate([dot32(packed, by_k[k].astype(F32), precision=HI) for k in range(top_k)], axis=0)
        score_parts += [both[:, i * tok : (i + 1) * tok] for i in range(per)]
    score_sum = score_parts[0]
    for j in range(1, n_dp):
        score_sum = score_sum + swap(score_parts[j], "dp", j)
    mixture = collect(results[0][0], results[1][0])
    d_chosen = score_sum - gates * jnp.sum(score_sum, axis=0, keepdims=True)
    d_logits = sum([picks[k] * d_chosen[k : k + 1] for k in range(top_k)])
    d_normed = back_sum + dot32(d_logits, w_router.astype(F32), ((0,), (1,)), precision=HI)
    cot_float = cotangent.astype(F32)
    d_stream = cot_float + inv_std * (
        d_normed
        - jnp.mean(d_normed, axis=1, keepdims=True)
        - normed * jnp.mean(d_normed * normed, axis=1, keepdims=True)
    )
    d_residual, late_stream = lax.optimization_barrier((d_stream.astype(BF), stream))
    layer_out = (late_stream + mixture).astype(BF)
    d_rel = jnp.concatenate([dot32(d_residual, piece, ((1,), (1,))).astype(BF) for piece in w_rel], axis=1)
    d_context = dot32(d_rel, reorder, ((1,), (1,))).astype(BF)

    rest, thirds = d_logits, []
    for _ in range(3):
        thirds.append(rest.astype(BF))
        rest = rest - thirds[-1].astype(F32)
    thirds = jnp.concatenate(thirds, axis=0)
    thirds = jnp.pad(thirds, ((0, -thirds.shape[0] % 128), (0, 0)))

    def sums_of(cols):
        return [
            dot32(ctx_rel[:, cols], d_residual, ((0,), (0,))),
            dot32(normed_rel[:, cols], thirds, ((0,), (1,))),
        ]

    half = width // 2
    sent = jnp.concatenate([v.astype(BF) for v in sums_of(slice(half, width))], axis=1)
    got = swap(sent, "expert", 1)
    part_out, part_router = sums_of(slice(0, half))
    part_out = part_out + got[:, :width].astype(F32)
    part_router = part_router + got[:, width:].astype(F32)
    bit = 2
    while bit < lo:
        half = half // 2
        sent = jnp.concatenate([part_out[half:], part_router[half:]], axis=1).astype(BF)
        got = swap(sent, "expert", bit).astype(F32)
        part_out, part_router = part_out[:half] + got[:, :width], part_router[:half] + got[:, width:]
        bit *= 2
    mid = width // 2
    left = [part_out[i * rows_q : (i + 1) * rows_q, :mid] for i in range(4)]
    right = [
        jnp.concatenate([part_out[i * rows_q : (i + 1) * rows_q, mid:], part_router[i * rows_q : (i + 1) * rows_q]], axis=1)
        for i in range(4)
    ]
    got_l = swap(jnp.concatenate([left[2], left[3]], axis=0).astype(BF), "expert", lo)
    got_r = swap(jnp.concatenate([right[1], right[3]], axis=0).astype(BF), "expert", hi)
    fin_l = swap((left[1] + got_l[rows_q:].astype(F32)).astype(BF), "expert", hi).astype(F32)
    fin_r = swap((right[2] + got_r[rows_q:].astype(F32)).astype(BF), "expert", lo).astype(F32)
    fin_l, fin_r = lax.optimization_barrier((fin_l, fin_r))
    kept = jnp.concatenate([left[0] + got_l[:rows_q].astype(F32) + fin_l, right[0] + got_r[:rows_q].astype(F32) + fin_r], axis=1)
    grads = kept[:shard]
    for j in range(1, n_dp):
        grads = grads + swap(kept[j * shard : (j + 1) * shard].astype(BF), "dp", j).astype(F32)
    grads = scale * grads
    grad_out = grads[:, :width]
    grad_router = sum([grads[:, width + i * experts : width + (i + 1) * experts] for i in range(3)])

    grad_fc1 = wgrad(scale, exp_dev, slot_in, [r[3] for r in results])
    grad_fc2 = wgrad(scale, exp_dev, [r[2] for r in results], slot_cot)
    return (layer_out, d_residual, d_context, grad_out, grad_router, grad_fc1, grad_fc2)


def solution(mesh):
    rows = P(("dp", "expert"), None)
    first = P("expert", None, "dp")
    second = P("expert", "dp", None)

    return jax.shard_map(
        on_device,
        mesh=mesh,
        in_specs=(rows, rows, rows, P(), rows, first, second, rows),
        out_specs=(rows, rows, rows, rows, rows, first, second),
        check_vma=False,
    )
```
